256 devices in a mesh: blk: 32 (over z, x_lo, core), head: 8 (over x_hi, y).
Axes of the slice: x: 4 (x_hi: 2, x_lo: 2; x = x_hi * 2 + x_lo), y: 4, z: 8, core: 2. Of those that a mesh axis runs over, the one named last changes fastest.
Arguments:
- query_tokens: bfloat16 [16384, 3072], P(('blk', 'head')), may hold values from -12 to 12
- key_tokens: bfloat16 [16384, 3072], P(('blk', 'head')), may hold values from -6 to 6
- value_tokens: bfloat16 [16384, 3072], P(('blk', 'head')), may hold values from -6 to 6
- out_weight: bfloat16 [3072, 3072], P('head'), may hold values from -1.75 to 1.75
- kv_blocks: int32 [128, 16], P('blk'), may hold values from -1 to 127, as said below
Outputs:
- projected: bfloat16 [16384, 3072], P(('blk', 'head'))
The draws below stay inside these ranges and needn't reach their ends.
Inputs may be any that keep to these rules, and one draw needn't show every extreme that they name: `kv_blocks`: row i lists the key blocks of 128 tokens that query block i attends to; let G = floor(i / 4). Entry 0 is i. Entry 1 is one of the blocks 4 * M to 4 * M + 3 with M = (G + 16) mod 32. Entry j >= 2 is -1 (absent) or one of the blocks 4 * (G + o) to 4 * (G + o) + 3, with o = j // 2 for even j and o = -(j - 1) // 2 for odd j; it is present whenever j < 8 and those blocks exist. Entries of one row are distinct.
All inputs are finite; a program needn't handle non-finite values.
Results may differ from the reference program's by a relative error of at most 0.012.
Values may be sent and summed in bfloat16 or wider, within the bound.
A program may use at most 128 MiB of HBM per device.

```python
import math
import jax
import jax.numpy as jnp
from jax import lax

HEADS = 24
HD = 128
D = 3072
BLOCK = 128
NSEL = 16
SEQ = 16384
QBLOCKS = 128
QBD = 4
N_HEAD = 8


def draw_query_tokens(key, part):
    drawn = jax.random.truncated_normal(jax.random.fold_in(key, 1), -6.0, 6.0, (SEQ, D), jnp.float32)
    return drawn.astype(jnp.bfloat16)


def draw_key_tokens(key, part):
    drawn = jax.random.truncated_normal(jax.random.fold_in(key, 2), -6.0, 6.0, (SEQ, D), jnp.float32)
    return drawn.astype(jnp.bfloat16)


def draw_kv_blocks(key, part):
    block_ids = jnp.arange(QBLOCKS, dtype=jnp.int32)
    groups = QBLOCKS // QBD
    owner = block_ids // QBD
    slot_ids = jnp.arange(NSEL, dtype=jnp.int32)
    offsets = slot_ids // 2 * jnp.where(slot_ids % 2 == 0, 1, -1)
    near_target = owner[:, None] + offsets[None, :]
    mirror = ((owner + groups // 2) % groups)[:, None]
    target = jnp.where(slot_ids[None, :] == 1, mirror, near_target)
    inside = jax.random.randint(jax.random.fold_in(key, 21), (QBLOCKS, NSEL), 0, QBD)
    chosen_block = jnp.where(slot_ids[None, :] == 0, block_ids[:, None], target * QBD + inside)
    counts = jax.random.randint(jax.random.fold_in(key, 22), (QBLOCKS, 1), NSEL // 2, NSEL + 1)
    present = (target >= 0) & (target < groups) & (slot_ids[None, :] < counts)
    return jnp.where(present, chosen_block, -1).astype(jnp.int32)


def steps_of(rng, dims, shards, low, top_value):
    loudness, own = 1.0, jax.random.fold_in(rng, 6)
    for dim, parts in shards:
        heights = jnp.exp(jax.random.uniform(jax.random.fold_in(own, dim), (parts,), jnp.float32, low / len(shards), top_value / len(shards)))
        loudness = loudness * jnp.repeat(heights, dims[dim] // parts).reshape([-1 if axis == dim else 1 for axis in range(len(dims))])
    return loudness


def normal_values(rng, extent, width, reach, shards=(), kind=jnp.bfloat16):
    result = width * jax.random.normal(rng, extent, jnp.float32)
    if shards:
        result = result * steps_of(rng, extent, shards, -0.22, 0.18)
    return jnp.clip(result, -reach, reach).astype(kind)


def setup_inputs(seed: int = 0) -> dict:
    splits = jax.random.split(jax.random.key(seed), 6)
    query_tokens = draw_query_tokens(jax.random.fold_in(splits[5], 71), 0)
    key_tokens = draw_key_tokens(jax.random.fold_in(splits[5], 71), 0)
    value_tokens = normal_values(splits[2], (SEQ, D), 1.0, 6.0, ((0, 256),))
    out_weight = normal_values(splits[3], (D, D), (D // 256) ** -0.5, 1.75, ((0, 8),))
    kv_blocks = draw_kv_blocks(jax.random.fold_in(splits[5], 71), 0)
    return {"query_tokens": query_tokens, "key_tokens": key_tokens, "value_tokens": value_tokens, "out_weight": out_weight, "kv_blocks": kv_blocks}


masked_low = -1e+30

def reference(query_tokens, key_tokens, value_tokens, out_weight, kv_blocks):
    query_blocks = query_tokens.reshape(QBLOCKS, BLOCK, HEADS, HD)
    key_blocks = key_tokens.reshape(QBLOCKS, BLOCK, HEADS, HD)
    value_blocks = value_tokens.reshape(QBLOCKS, BLOCK, HEADS, HD)
    scaling = 1.0 / math.sqrt(HD)

    def one_block(block_index):
        listed = kv_blocks[block_index]
        present = listed >= 0
        safe_index = jnp.maximum(listed, 0).astype(jnp.int32)
        keys_here = key_blocks[safe_index].astype(jnp.float32)
        values_here = value_blocks[safe_index].astype(jnp.float32)
        queries_here = query_blocks[block_index].astype(jnp.float32)
        scores = jnp.einsum('qhd,nkhd->hqnk', queries_here, keys_here) * scaling
        allowed = present[None, None, :, None]
        peak_value = lax.optimization_barrier(jnp.max(jnp.where(allowed, scores, masked_low), axis=(2, 3), keepdims=True))
        weights = jnp.where(allowed, jnp.exp(scores - peak_value), 0.0)
        denom = lax.optimization_barrier(jnp.sum(weights, axis=(2, 3)))
        probs = lax.optimization_barrier(weights.astype(jnp.bfloat16)).astype(jnp.float32)
        outputs = jnp.einsum('hqnk,nkhd->hqd', probs, values_here) / denom[..., None]
        return jnp.transpose(outputs, (1, 0, 2)).reshape(BLOCK, D).astype(jnp.bfloat16)
    attended = lax.map(one_block, jnp.arange(QBLOCKS, dtype=jnp.int32)).reshape(SEQ, D)
    group_width = D // N_HEAD
    running_sum = jnp.zeros((SEQ, D), jnp.float32)
    for group in range(N_HEAD):
        partial_term = jnp.dot(attended[:, group * group_width:(group + 1) * group_width], out_weight[group * group_width:(group + 1) * group_width], preferred_element_type=jnp.float32).astype(jnp.bfloat16)
        running_sum = running_sum + lax.optimization_barrier(partial_term).astype(jnp.float32)
    return running_sum.astype(jnp.bfloat16)
```

```python
import functools
import math

import jax
import jax.numpy as jnp
from jax import lax
from jax.experimental import pallas as pl
from jax.experimental.pallas import tpu as pltpu
from jax.sharding import PartitionSpec as P

HD = 128
BLK = 128
HEADS_DEV = 3
MESH = pl.DeviceIdType.MESH
ABSENT = -(2.0**100)
SCALE = 1.0 / math.sqrt(HD)

OWN, M1, P1, M2, P2, MIR, TMP = range(7)
UP = {1: M1, 2: M2, 3: TMP, 4: MIR}
DOWN = {1: P1, 2: P2, 3: TMP, 4: MIR}
ORDER = [
    ("A", 0, 1), ("B", 0, 1), ("A", 0, 2), ("B", 0, 2), ("A", 0, 3), ("A", 1, 1),
    ("A", 0, 4), ("B", 1, 1), ("A", 1, 2), ("B", 1, 2), ("A", 1, 3), ("A", 2, 1),
    ("A", 1, 4), ("B", 2, 1), ("A", 2, 2), ("B", 2, 2), ("A", 2, 3), ("A", 2, 4),
]
WORK = {
    8: [("unit", 0, 3)], 9: [("unit", 0, 2)], 10: [("unit", 0, 1)], 11: [("unit", 0, 0)],
    13: [("merge", 0)],
    14: [("unit", 1, 3)], 15: [("unit", 1, 2)], 16: [("unit", 1, 1)],
    17: [("unit", 1, 0), ("merge", 1), ("unit", 2, 3), ("unit", 2, 2), ("unit", 2, 1), ("unit", 2, 0), ("merge", 2)],
}


def kernel(q_hbm, k_hbm, v_hbm, kvb_ref, out_ref, *scratch):
    nh = HEADS_DEV
    kb, vb, qb_, os_, or_ = (scratch[i * nh : (i + 1) * nh] for i in range(5))
    kvb_all, kvb_smem, a_send, a_recv, zs, zr, qs, qr, osem, orsem, misc = scratch[5 * nh :]
    b = lax.axis_index("blk")
    g = lax.axis_index("head")
    z, r = lax.div(b, 4), lax.rem(b, 4)
    xl, c = lax.div(r, 2), lax.rem(r, 2)
    ghalf, glow = lax.div(g, 2), lax.rem(g, 2)
    plane = [(xl, c), (xl, 1 - c), (1 - xl, c), (1 - xl, 1 - c)]
    plane_r = [x * 2 + cc for x, cc in plane]
    plane_dev = [(z * 4 + rr, g) for rr in plane_r]
    zdev = {"U": (lax.rem(z + 1, 8) * 4 + r, g), "D": (lax.rem(z + 7, 8) * 4 + r, g)}

    def head_dev(d):
        return lax.rem(g + d, 8)

    barrier = pltpu.get_barrier_semaphore()
    for dev in plane_dev[1:] + list(zdev.values()) + [(b, head_dev(d)) for d in range(1, 8)]:
        pl.semaphore_signal(barrier, inc=1, device_id=dev, device_id_type=MESH)
    pl.semaphore_wait(barrier, 12)

    def wait_bytes(ref, sem):
        pltpu.make_async_copy(ref, ref, sem).wait()

    done = set()

    src = {"K": k_hbm, "V": v_hbm, "Q": q_hbm}

    def a2a_dst(x, h):
        if x == "Q":
            return qb_[h], r * 4
        return (kb if x == "K" else vb)[h], OWN * 4

    a2a_idx = {}
    for h in range(nh):
        for x in "KVQ":
            a2a_idx[x, h] = len(a2a_idx)

    def a2a_start(x, h):
        i = a2a_idx[x, h]
        buf, base = a2a_dst(x, h)
        dst = buf.at[base + ghalf, pl.ds(pl.multiple_of(glow * 64, 64), 64), :]

        def cols(dest):
            return src[x].at[:, pl.ds(pl.multiple_of(dest * (nh * HD) + h * HD, HD), HD)]

        pltpu.make_async_copy(cols(g), dst, a_recv.at[i]).start()

        def one(d, carry):
            dest = head_dev(d)
            pltpu.make_async_remote_copy(
                src_ref=cols(dest), dst_ref=dst, send_sem=a_send.at[i], recv_sem=a_recv.at[i],
                device_id=(b, dest), device_id_type=MESH,
            ).start()
            return carry

        lax.fori_loop(1, 8, one, 0)

    def a2a_wait(x, h):
        if ("a2a", x, h) in done:
            return
        done.add(("a2a", x, h))
        buf, base = a2a_dst(x, h)
        wait_bytes(buf.at[pl.ds(base, 4)], a_recv.at[a2a_idx[x, h]])

    kv_copies = []
    for i in range(1, 4):
        kv_copies.append(
            pltpu.make_async_remote_copy(
                src_ref=kvb_ref, dst_ref=kvb_all.at[r], send_sem=misc.at[2 * i], recv_sem=misc.at[2 * i + 1],
                device_id=plane_dev[i], device_id_type=MESH,
            )
        )
    kv_own = pltpu.make_async_copy(kvb_ref, kvb_all.at[r], misc.at[0])

    for x, h in list(a2a_idx)[:2]:
        a2a_start(x, h)
    kv_own.start()
    for cp in kv_copies:
        cp.start()
    for x, h in list(a2a_idx)[2:]:
        a2a_start(x, h)

    def tensor(direction, kind):
        return kb if (direction == "U") == (kind == "A") else vb

    zname = {}

    def zcopy(direction, n):
        kind, h, hop = ORDER[n]
        slots = UP if direction == "U" else DOWN
        buf = tensor(direction, kind)[h]
        s_src = OWN if hop == 1 else slots[hop - 1]
        s_dst = slots[hop]
        k = n + (len(ORDER) if direction == "D" else 0)
        return pltpu.make_async_remote_copy(
            src_ref=buf.at[pl.ds(s_src * 4, 4)], dst_ref=buf.at[pl.ds(s_dst * 4, 4)],
            send_sem=zs.at[k], recv_sem=zr.at[k], device_id=zdev[direction], device_id_type=MESH,
        )

    def z_wait(direction, n):
        if ("z", direction, n) in done:
            return
        done.add(("z", direction, n))
        zcopy(direction, n).wait_recv()

    def z_step(direction, n):
        kind, h, hop = ORDER[n]
        if hop == 1:
            is_k = (direction == "U") == (kind == "A")
            a2a_wait("K" if is_k else "V", h)
        else:
            z_wait(direction, ORDER.index((kind, h, hop - 1)))
        zcopy(direction, n).start()

    def q_copy(h, i):
        ref = qb_[h].at[pl.ds(r * 4, 4)]
        return pltpu.make_async_remote_copy(
            src_ref=ref, dst_ref=ref, send_sem=qs.at[h * 3 + i - 1], recv_sem=qr.at[h * 3 + i - 1],
            device_id=plane_dev[i], device_id_type=MESH,
        )

    def q_send(h):
        a2a_wait("Q", h)
        for i in (3, 2, 1):
            q_copy(h, i).start()

    def q_wait(h):
        if ("q", h) in done:
            return
        done.add(("q", h))
        for i in (1, 2, 3):
            ref = qb_[h].at[pl.ds(plane_r[i] * 4, 4)]
            wait_bytes(ref, qr.at[h * 3 + i - 1])

    def kvb_wait():
        if "kvb" in done:
            return
        done.add("kvb")
        kv_own.wait()
        for i in range(1, 4):
            kv_copies[i - 1].wait()
        cp = pltpu.make_async_copy(kvb_all, kvb_smem, misc.at[1])
        cp.start()
        cp.wait()

    lane = lax.broadcasted_iota(jnp.int32, (BLK, BLK), 1)

    def o_copy(h, i):
        return pltpu.make_async_remote_copy(
            src_ref=os_[h].at[i], dst_ref=or_[h].at[i], send_sem=osem.at[h * 4 + i], recv_sem=orsem.at[h * 4 + i],
            device_id=plane_dev[i], device_id_type=MESH,
        )

    def unit(h, i):
        kvb_wait()
        q_wait(h)
        for x in "KV":
            a2a_wait(x, h)
        for n, (_, hh, _) in enumerate(ORDER):
            if hh == h:
                z_wait("U", n)
                z_wait("D", n)
        rq = plane_r[i]
        dl = r - rq
        gt = lax.div(dl + 3, 4)
        lt = lax.div(3 - dl, 4)
        eq = 1 - gt - lt
        picks = [
            (OWN, gt * (2 * dl) + lt * (1 - 2 * dl)),
            (M1, 9 - 2 * dl),
            (P1, 2 * dl + 8),
            (M2 * gt + P2 * lt + MIR * eq, gt * (17 - 2 * dl) + lt * (2 * dl + 16) + eq),
        ]

        def block(j, stats):
            q = qb_[h][rq * 4 + j]
            scores, vals = [], []
            for slot, col in picks:
                e = kvb_smem[rq, j, col]
                idx = slot * 4 + jnp.bitwise_and(e, 3)
                bias = jnp.where(e >= 0, 0.0, ABSENT).astype(jnp.float32)
                s = lax.dot_general(q, kb[h][idx], (((1,), (1,)), ((), ())), preferred_element_type=jnp.float32)
                scores.append(s * SCALE + bias)
                vals.append(vb[h][idx])
            top = functools.reduce(jnp.maximum, scores)
            m = jnp.max(top, axis=1, keepdims=True).astype(jnp.bfloat16).astype(jnp.float32)
            ps = [jnp.exp(s - m) for s in scores]
            l = jnp.sum(functools.reduce(jnp.add, ps), axis=1, keepdims=True)
            o = functools.reduce(
                jnp.add,
                [
                    jnp.dot(p.astype(jnp.bfloat16), v, preferred_element_type=jnp.float32)
                    for p, v in zip(ps, vals)
                ],
            )
            os_[h][i, j] = o.astype(jnp.bfloat16)
            l_hi = l.astype(jnp.bfloat16).astype(jnp.float32)
            stats = jnp.where(lane == j, m, stats)
            stats = jnp.where(lane == j + 4, l_hi, stats)
            return jnp.where(lane == j + 8, l - l_hi, stats)

        stats = lax.fori_loop(0, 4, block, jnp.zeros((BLK, BLK), jnp.float32))
        os_[h][i, 4] = stats.astype(jnp.bfloat16)
        if i:
            o_copy(h, i).start()

    def merge(h):
        for i in (1, 2, 3):
            o_copy(h, i).wait_recv()
        bufs = [os_[h].at[0]] + [or_[h].at[i] for i in (1, 2, 3)]
        stats = [bf[4].astype(jnp.float32) for bf in bufs]
        for j in range(4):
            ms = [s[:, j : j + 1] for s in stats]
            ls = [s[:, j + 4 : j + 5] + s[:, j + 8 : j + 9] for s in stats]
            top = functools.reduce(jnp.maximum, ms)
            ws = [jnp.exp(m - top) for m in ms]
            inv = 1.0 / functools.reduce(jnp.add, [w * l for w, l in zip(ws, ls)])
            o = functools.reduce(
                jnp.add, [(w * inv) * bf[j].astype(jnp.float32) for w, bf in zip(ws, bufs)]
            )
            out_ref[j * BLK : (j + 1) * BLK, h * HD : (h + 1) * HD] = o.astype(jnp.bfloat16)

    for n in range(len(ORDER)):
        z_step("U", n)
        z_step("D", n)
        if n in (3, 7, 11):
            q_send((n - 3) // 4)
        for job in WORK.get(n, ()):
            if job[0] == "unit":
                unit(job[1], job[2])
            else:
                merge(job[1])

    for n in range(len(ORDER)):
        for direction in "UD":
            zcopy(direction, n).wait_send()
    for h in range(nh):
        for i in (1, 2, 3):
            q_copy(h, i).wait_send()
            o_copy(h, i).wait_send()
    for (x, h), i in a2a_idx.items():
        wait_bytes(src[x].at[:, pl.ds(0, 7 * HD)], a_send.at[i])


def on_device(query_tokens, key_tokens, value_tokens, out_weight, kv_blocks):
    nh = HEADS_DEV
    rows = query_tokens.shape[0] * 8
    lists = jnp.pad(kv_blocks, ((0, 4), (0, 128 - kv_blocks.shape[1])), constant_values=-1)
    any_spec = pl.BlockSpec(memory_space=pl.ANY)
    vm = pl.BlockSpec(memory_space=pltpu.VMEM)
    bf = jnp.bfloat16
    dma = pltpu.SemaphoreType.DMA
    attended = pl.pallas_call(
        kernel,
        out_shape=jax.ShapeDtypeStruct((rows, nh * HD), bf),
        in_specs=[any_spec, any_spec, any_spec, vm],
        out_specs=vm,
        scratch_shapes=[pltpu.VMEM((28, BLK, HD), bf)] * (2 * nh)
        + [pltpu.VMEM((16, BLK, HD), bf)] * nh
        + [pltpu.VMEM((4, 5, BLK, HD), bf)] * (2 * nh)
        + [
            pltpu.VMEM((4, 8, 128), jnp.int32),
            pltpu.SMEM((4, 8, 128), jnp.int32),
            dma((9,)), dma((9,)),
            dma((36,)), dma((36,)),
            dma((9,)), dma((9,)),
            dma((12,)), dma((12,)),
            dma((8,)),
        ],
        compiler_params=pltpu.CompilerParams(
            collective_id=0, has_side_effects=True, vmem_limit_bytes=48 << 20
        ),
        name="attend",
    )(query_tokens, key_tokens, value_tokens, lists)
    return lax.psum_scatter(
        jnp.dot(attended, out_weight, preferred_element_type=jnp.float32).astype(jnp.bfloat16),
        "head",
        scatter_dimension=0,
        tiled=True,
    )


def solution(mesh):
    placed = (
        P(("blk", "head"), None),
        P(("blk", "head"), None),
        P(("blk", "head"), None),
        P("head", None),
        P("blk", None),
    )
    return jax.shard_map(
        on_device, mesh=mesh, in_specs=placed, out_specs=P(("blk", "head"), None), check_vma=False
    )
```

```python
import functools
import math

import jax
import jax.numpy as jnp
from jax import lax
from jax.experimental import pallas as pl
from jax.experimental.pallas import tpu as pltpu
from jax.sharding import PartitionSpec as P

HD = 128
BLK = 128
HEADS_DEV = 3
MESH = pl.DeviceIdType.MESH
ABSENT = -(2.0**100)
SCALE = 1.0 / math.sqrt(HD)

OWN, M1, P1, M2, P2, MIR, TMP = range(7)
UP = {1: M1, 2: M2, 3: TMP, 4: MIR}
DOWN = {1: P1, 2: P2, 3: TMP, 4: MIR}
ORDER = [
    ("A", 0, 1), ("B", 0, 1), ("A", 0, 2), ("B", 0, 2), ("A", 1, 1), ("A", 0, 3),
    ("B", 1, 1), ("A", 1, 2), ("A", 0, 4), ("B", 1, 2), ("A", 1, 3), ("A", 2, 1),
    ("A", 1, 4), ("B", 2, 1), ("A", 2, 2), ("B", 2, 2), ("A", 2, 3), ("A", 2, 4),
]
WORK = {
    0: ["a2a Q0", "a2a K1", "a2a V1"],
    1: ["a2a K2", "a2a V2", "a2a Q1", "a2a Q2", "wown", "w1 2", "xo0"],
    2: ["qsend 0"],
    3: ["w1 0", "qfwd 0"],
    6: ["unit 0 3", "unit 0 2", "qsend 1"],
    7: ["unit 0 1", "qfwd 1"],
    8: ["w1r 2", "w1 1"],
    9: ["xor 0", "qsend 2"],
    10: ["qfwd 2"],
    11: ["unit 0 0", "merge 0", "w1r 0", "unit 1 3", "unit 1 2"],
    12: ["unit 1 1", "w2r 2"],
    14: ["w1r 1", "unit 1 0", "merge 1"],
    15: ["w2r 0", "xor 1", "xor 2"],
    16: ["unit 2 3", "unit 2 2", "xor 3"],
    17: ["unit 2 1", "w2r 1", "proj 0", "proj 1", "unit 2 0", "merge 2", "final"],
}


def kernel(q_hbm, k_hbm, v_hbm, w_hbm, kvb_ref, out_ref, *scratch):
    nh = HEADS_DEV
    kb, vb, qb_, os_, or_, wb, att, ab, km, vm = (scratch[i * nh : (i + 1) * nh] for i in range(10))
    (kvb_all, kvb_smem, pacc, pb, prec, a_send, a_recv, zs, zr, qs, qr, osem, orsem, misc, ws, wr, ts, tr) = scratch[10 * nh :]
    b = lax.axis_index("blk")
    g = lax.axis_index("head")
    z, r = lax.div(b, 4), lax.rem(b, 4)
    xl, c = lax.div(r, 2), lax.rem(r, 2)
    ghalf, glow = lax.div(g, 2), lax.rem(g, 2)
    plane = [(xl, c), (xl, 1 - c), (1 - xl, c), (1 - xl, 1 - c)]
    plane_r = [x * 2 + cc for x, cc in plane]
    plane_dev = [(z * 4 + rr, g) for rr in plane_r]
    xh, y = lax.div(g, 4), lax.rem(g, 4)
    xo_dev = (z * 4 + (1 - xl) * 2 + c, (1 - xh) * 4 + y)
    xh_dev = (b, (1 - xh) * 4 + y)
    zdev = {"U": (lax.rem(z + 1, 8) * 4 + r, g), "D": (lax.rem(z + 7, 8) * 4 + r, g)}

    def head_dev(d):
        return lax.rem(g + d, 8)

    barrier = pltpu.get_barrier_semaphore()
    for dev in plane_dev[1:] + list(zdev.values()) + [(b, head_dev(d)) for d in range(1, 8)] + [xo_dev]:
        pl.semaphore_signal(barrier, inc=1, device_id=dev, device_id_type=MESH)
    pl.semaphore_wait(barrier, 13)

    def wait_bytes(ref, sem):
        pltpu.make_async_copy(ref, ref, sem).wait()

    done = set()

    src = {"K": k_hbm, "V": v_hbm, "Q": q_hbm}

    def a2a_dst(x, h):
        if x == "Q":
            return qb_[h], r * 4
        return (kb if x == "K" else vb)[h], OWN * 4

    a2a_idx = {}
    for h in range(nh):
        for x in "KVQ":
            a2a_idx[x, h] = len(a2a_idx)

    def a2a_start(x, h):
        i = a2a_idx[x, h]
        buf, base = a2a_dst(x, h)
        dst = buf.at[base + ghalf, pl.ds(pl.multiple_of(glow * 64, 64), 64), :]

        def cols(dest):
            return src[x].at[:, pl.ds(pl.multiple_of(dest * (nh * HD) + h * HD, HD), HD)]

        pltpu.make_async_copy(cols(g), dst, a_recv.at[i]).start()

        def one(d, carry):
            dest = head_dev(d)
            pltpu.make_async_remote_copy(
                src_ref=cols(dest), dst_ref=dst, send_sem=a_send.at[i], recv_sem=a_recv.at[i],
                device_id=(b, dest), device_id_type=MESH,
            ).start()
            return carry

        lax.fori_loop(1, 8, one, 0)

    def a2a_wait(x, h):
        if ("a2a", x, h) in done:
            return
        done.add(("a2a", x, h))
        buf, base = a2a_dst(x, h)
        wait_bytes(buf.at[pl.ds(base, 4)], a_recv.at[a2a_idx[x, h]])

    kv_copies = []
    for i in range(1, 4):
        kv_copies.append(
            pltpu.make_async_remote_copy(
                src_ref=kvb_ref, dst_ref=kvb_all.at[r], send_sem=misc.at[2 * i], recv_sem=misc.at[2 * i + 1],
                device_id=plane_dev[i], device_id_type=MESH,
            )
        )
    kv_own = pltpu.make_async_copy(kvb_ref, kvb_all.at[r], misc.at[0])

    for x, h in list(a2a_idx)[:2]:
        a2a_start(x, h)
    kv_own.start()
    for cp in kv_copies:
        cp.start()

    def tensor(direction, kind):
        return (kb, km) if (direction == "U") == (kind == "A") else (vb, vm)

    def slot_ref(bufs, h, slot):
        return bufs[0][h].at[pl.ds(slot * 4, 4)] if slot < MIR else bufs[1][h].at[pl.ds((slot - MIR) * 4, 4)]

    zname = {}

    def zcopy(direction, n):
        kind, h, hop = ORDER[n]
        slots = UP if direction == "U" else DOWN
        bufs = tensor(direction, kind)
        s_src = OWN if hop == 1 else slots[hop - 1]
        s_dst = slots[hop]
        k = n + (len(ORDER) if direction == "D" else 0)
        return pltpu.make_async_remote_copy(
            src_ref=slot_ref(bufs, h, s_src), dst_ref=slot_ref(bufs, h, s_dst),
            send_sem=zs.at[k], recv_sem=zr.at[k], device_id=zdev[direction], device_id_type=MESH,
        )

    def z_wait(direction, n):
        if ("z", direction, n) in done:
            return
        done.add(("z", direction, n))
        zcopy(direction, n).wait_recv()

    def z_step(direction, n):
        kind, h, hop = ORDER[n]
        if hop == 1:
            is_k = (direction == "U") == (kind == "A")
            a2a_wait("K" if is_k else "V", h)
        else:
            z_wait(direction, ORDER.index((kind, h, hop - 1)))
        zcopy(direction, n).start()

    def q_copy(h, i):
        ref = qb_[h].at[pl.ds(plane_r[2 if i == 3 else 0] * 4, 4)]
        return pltpu.make_async_remote_copy(
            src_ref=ref, dst_ref=ref, send_sem=qs.at[h * 3 + i - 1], recv_sem=qr.at[h * 3 + i - 1],
            device_id=plane_dev[2 if i == 2 else 1], device_id_type=MESH,
        )

    def q_send(h):
        a2a_wait("Q", h)
        for i in (2, 1):
            q_copy(h, i).start()

    def q_fwd(h):
        q_wait(h, (2,))
        q_copy(h, 3).start()

    def q_wait(h, which=(1, 2, 3)):
        for i in which:
            if ("q", h, i) not in done:
                done.add(("q", h, i))
                wait_bytes(qb_[h].at[pl.ds(plane_r[i] * 4, 4)], qr.at[h * 3 + i - 1])

    def kvb_wait():
        if "kvb" in done:
            return
        done.add("kvb")
        kv_own.wait()
        for i in range(1, 4):
            kv_copies[i - 1].wait()
        cp = pltpu.make_async_copy(kvb_all, kvb_smem, misc.at[1])
        cp.start()
        cp.wait()

    lane = lax.broadcasted_iota(jnp.int32, (BLK, BLK), 1)

    def o_copy(h, i):
        return pltpu.make_async_remote_copy(
            src_ref=os_[h].at[i], dst_ref=or_[h].at[i], send_sem=osem.at[h * 4 + i], recv_sem=orsem.at[h * 4 + i],
            device_id=plane_dev[i], device_id_type=MESH,
        )

    def unit(h, i):
        kvb_wait()
        q_wait(h)
        for x in "KV":
            a2a_wait(x, h)
        for n, (_, hh, hop) in enumerate(ORDER):
            if hh == h and hop in ((1, 2, 4) if i == 0 else (1, 2)):
                z_wait("U", n)
                z_wait("D", n)
        rq = plane_r[i]
        dl = r - rq
        gt = lax.div(dl + 3, 4)
        lt = lax.div(3 - dl, 4)
        eq = 1 - gt - lt
        picks = [
            (OWN, gt * (2 * dl) + lt * (1 - 2 * dl)),
            (M1, 9 - 2 * dl),
            (P1, 2 * dl + 8),
            (0 if i == 0 else M2 * gt + P2 * lt, gt * (17 - 2 * dl) + lt * (2 * dl + 16) + eq),
        ]

        def block(j, stats):
            q = qb_[h][rq * 4 + j]
            scores, vals = [], []
            for n, (slot, col) in enumerate(picks):
                keys, values = (km[h], vm[h]) if n == 3 and i == 0 else (kb[h], vb[h])
                e = kvb_smem[rq, j, col]
                idx = slot * 4 + jnp.bitwise_and(e, 3)
                bias = jnp.where(e >= 0, 0.0, ABSENT).astype(jnp.float32)
                s = lax.dot_general(q, keys[idx], (((1,), (1,)), ((), ())), preferred_element_type=jnp.float32)
                scores.append(s * SCALE + bias)
                vals.append(values[idx])
            top = functools.reduce(jnp.maximum, scores)
            m = jnp.max(top, axis=1, keepdims=True).astype(jnp.bfloat16).astype(jnp.float32)
            ps = [jnp.exp(s - m) for s in scores]
            l = jnp.sum(functools.reduce(jnp.add, ps), axis=1, keepdims=True)
            o = functools.reduce(
                jnp.add,
                [
                    jnp.dot(p.astype(jnp.bfloat16), v, preferred_element_type=jnp.float32)
                    for p, v in zip(ps, vals)
                ],
            )
            os_[h][i, j] = o.astype(jnp.bfloat16)
            l_hi = l.astype(jnp.bfloat16).astype(jnp.float32)
            stats = jnp.where(lane == j, m, stats)
            stats = jnp.where(lane == j + 4, l_hi, stats)
            return jnp.where(lane == j + 8, l - l_hi, stats)

        stats = lax.fori_loop(0, 4, block, jnp.zeros((BLK, BLK), jnp.float32))
        os_[h][i, 4] = stats.astype(jnp.bfloat16)
        if i:
            o_copy(h, i).start()

    def merge(h):
        for i in (1, 2, 3):
            o_copy(h, i).wait_recv()
        bufs = [os_[h].at[0]] + [or_[h].at[i] for i in (1, 2, 3)]
        stats = [bf[4].astype(jnp.float32) for bf in bufs]
        for j in range(4):
            ms = [s[:, j : j + 1] for s in stats]
            ls = [s[:, j + 4 : j + 5] + s[:, j + 8 : j + 9] for s in stats]
            top = functools.reduce(jnp.maximum, ms)
            ws = [jnp.exp(m - top) for m in ms]
            inv = 1.0 / functools.reduce(jnp.add, [w * l for w, l in zip(ws, ls)])
            o = functools.reduce(
                jnp.add, [(w * inv) * bf[j].astype(jnp.float32) for w, bf in zip(ws, bufs)]
            )
            att[h][j * BLK : (j + 1) * BLK, :] = o.astype(jnp.bfloat16)
        att_copies(h)

    def att_copies(h):
        def rows(gg):
            return att[h].at[pl.ds(pl.multiple_of(gg * 64, 64), 64), :]

        if h < 2:
            col = pl.ds(pl.multiple_of(y * HD, HD), HD)
            for p in range(2):
                dst = ab[h].at[p, :, col]
                pltpu.make_async_copy(rows(p * 4 + y), dst, tr.at[h]).start()
                for d in (2, 1, 3):
                    yy = lax.rem(y + d, 4)
                    pltpu.make_async_remote_copy(
                        src_ref=rows(p * 4 + yy), dst_ref=dst, send_sem=ts.at[h], recv_sem=tr.at[h],
                        device_id=(b, xh * 4 + yy), device_id_type=MESH,
                    ).start()
        else:
            dst = ab[h].at[:, pl.ds(pl.multiple_of(g * HD, HD), HD)]
            pltpu.make_async_copy(rows(g), dst, tr.at[h]).start()
            for d in range(1, 8):
                gg = head_dev(d)
                pltpu.make_async_remote_copy(
                    src_ref=rows(gg), dst_ref=dst, send_sem=ts.at[h], recv_sem=tr.at[h],
                    device_id=(b, gg), device_id_type=MESH,
                ).start()

    half = w_hbm.shape[1] // 2
    wcol = pl.ds(pl.multiple_of(c * half, 128), half)
    ocol = pl.ds(pl.multiple_of((1 - c) * half, 128), half)
    ydev = {d: (b, xh * 4 + lax.rem(y + d, 4)) for d in (1, 2, 3)}

    def widx(h, d, other=False):
        base = 0 if h < 2 else (1 - xh if other else xh) * 4
        return base + lax.rem(y + d, 4)

    def remote(src_ref, dst_ref, i, dev):
        return pltpu.make_async_remote_copy(
            src_ref=src_ref, dst_ref=dst_ref, send_sem=ws.at[i], recv_sem=wr.at[i], device_id=dev, device_id_type=MESH
        )

    def w_hop1(h, d):
        return remote(
            w_hbm.at[h * HD : (h + 1) * HD, wcol], wb[h].at[widx(h, 0), :, wcol], h * 7 + (0 if d == 1 else 1), ydev[d]
        )

    def w_hop2(h, d):
        ref = wb[h].at[widx(h, 4 - d), pl.ds(0 if d == 1 else 64, 64), wcol]
        return remote(ref, ref, h * 7 + (2 if d == 1 else 3), ydev[d])

    def w_sib(h, d):
        ref = wb[h].at[widx(h, d), :, wcol]
        return remote(ref, ref, h * 7 + 3 + d, plane_dev[1])

    def x_piece(k):
        dst = wb[2].at[widx(2, k), :, wcol]
        return remote(w_hbm.at[2 * HD : 3 * HD, wcol] if k == 0 else dst, dst, 21 + k, xo_dev)

    def x_sib(k):
        ref = wb[2].at[widx(2, k, True), :, wcol]
        return remote(ref, ref, 25 + k, plane_dev[1])

    def w_own(h):
        return pltpu.make_async_copy(w_hbm.at[h * HD : (h + 1) * HD, :], wb[h].at[widx(h, 0)], tr.at[3 + h])

    wsends = []

    def go(cp):
        cp.start()
        wsends.append(cp)

    def w_ready(h):
        w_own(h).wait()
        for d in (1, 2, 3):
            wait_bytes(wb[h].at[widx(h, d), :, ocol], wr.at[h * 7 + 3 + d])
        if h == 2:
            for k in range(4):
                wait_bytes(wb[2].at[widx(2, k, True), :, ocol], wr.at[25 + k])

    step = 512

    def columns(t):
        return pl.ds(pl.multiple_of(t * step, step), step)

    def project(h):
        w_ready(h)
        wait_bytes(ab[h], tr.at[h])
        rows = ab[h][...].reshape(2 * 64, 4 * HD)

        def one(t, carry):
            col = columns(t)
            res = jnp.dot(rows, wb[h][:, :, col].reshape(4 * HD, step), preferred_element_type=jnp.float32)
            if h:
                res = res + pacc[:, col]
                pb[:, col] = res.astype(jnp.bfloat16)
            pacc[:, col] = res
            return carry

        lax.fori_loop(0, pacc.shape[1] // step, one, 0)
        if h:
            p_copy.start()

    p_copy = pltpu.make_async_remote_copy(
        src_ref=pb.at[pl.ds(pl.multiple_of((1 - xh) * 64, 64), 64), :], dst_ref=prec,
        send_sem=ts.at[3], recv_sem=tr.at[6], device_id=xh_dev, device_id_type=MESH,
    )

    def final():
        w_ready(2)
        wait_bytes(ab[2], tr.at[2])
        p_copy.wait_recv()
        rows = ab[2][...]

        def one(t, carry):
            col = columns(t)
            res = jnp.dot(rows, wb[2][:, :, col].reshape(8 * HD, step), preferred_element_type=jnp.float32)
            mine = pacc[pl.ds(pl.multiple_of(xh * 64, 64), 64), col]
            out_ref[:, col] = (res + mine + prec[:, col].astype(jnp.float32)).astype(jnp.bfloat16)
            return carry

        lax.fori_loop(0, pacc.shape[1] // step, one, 0)

    def job(text):
        name, *rest = text.split(" ")
        if name == "a2a":
            a2a_start(rest[0][0], int(rest[0][1]))
            return
        v = [int(a) for a in rest]
        if name == "unit":
            unit(*v)
        elif name == "merge":
            merge(*v)
        elif name == "proj":
            project(*v)
        elif name == "final":
            final()
        elif name == "qsend":
            q_send(*v)
        elif name == "qfwd":
            q_fwd(*v)
        elif name == "wown":
            for h in range(nh):
                w_own(h).start()
        elif name == "w1":
            go(w_hop1(v[0], 1))
            go(w_hop1(v[0], 3))
        elif name == "w1r":
            h = v[0]
            w_hop1(h, 1).wait_recv()
            w_hop1(h, 3).wait_recv()
            go(w_hop2(h, 1))
            go(w_hop2(h, 3))
            go(w_sib(h, 1))
            go(w_sib(h, 3))
            if h == 2:
                go(x_piece(1))
                go(x_piece(3))
        elif name == "w2r":
            h = v[0]
            w_hop2(h, 1).wait_recv()
            w_hop2(h, 3).wait_recv()
            go(w_sib(h, 2))
            if h == 2:
                go(x_piece(2))
        elif name == "xo0":
            go(x_piece(0))
        elif name == "xor":
            k = (0, 1, 3, 2)[v[0]]
            x_piece(k).wait_recv()
            go(x_sib(k))

    for n in range(len(ORDER)):
        z_step("U", n)
        z_step("D", n)
        for text in WORK.get(n, ()):
            job(text)

    for n in range(len(ORDER)):
        for direction in "UD":
            zcopy(direction, n).wait_send()
    for h in range(nh):
        for i in (1, 2, 3):
            q_copy(h, i).wait_send()
            o_copy(h, i).wait_send()
    for (x, h), i in a2a_idx.items():
        wait_bytes(src[x].at[:, pl.ds(0, 7 * HD)], a_send.at[i])
    for cp in wsends:
        cp.wait_send()
    wait_bytes(att[0].at[pl.ds(0, 6 * 64)], ts.at[0])
    wait_bytes(att[1].at[pl.ds(0, 6 * 64)], ts.at[1])
    wait_bytes(att[2].at[pl.ds(0, 7 * 64)], ts.at[2])
    p_copy.wait_send()


def on_device(query_tokens, key_tokens, value_tokens, out_weight, kv_blocks):
    nh = HEADS_DEV
    rows, width = query_tokens.shape
    lists = jnp.pad(kv_blocks, ((0, 4), (0, 128 - kv_blocks.shape[1])), constant_values=-1)
    any_spec = pl.BlockSpec(memory_space=pl.ANY)
    vm = pl.BlockSpec(memory_space=pltpu.VMEM)
    bf = jnp.bfloat16
    dma = pltpu.SemaphoreType.DMA
    return pl.pallas_call(
        kernel,
        out_shape=jax.ShapeDtypeStruct((rows, width), bf),
        in_specs=[any_spec, any_spec, any_spec, any_spec, vm],
        out_specs=vm,
        scratch_shapes=[pltpu.VMEM((20, BLK, HD), bf)] * (2 * nh)
        + [pltpu.VMEM((16, BLK, HD), bf)] * nh
        + [pltpu.VMEM((4, 5, BLK, HD), bf)] * (2 * nh)
        + [pltpu.VMEM((n, HD, width), bf) for n in (4, 4, 8)]
        + [pltpu.VMEM((8 * rows, HD), bf)] * nh
        + [pltpu.VMEM((2, rows, 4 * HD), bf)] * 2
        + [pltpu.VMEM((rows, 8 * HD), bf)]
        + [pltpu.VMEM((8, BLK, HD), bf)] * (2 * nh)
        + [
            pltpu.VMEM((4, 8, 128), jnp.int32),
            pltpu.SMEM((4, 8, 128), jnp.int32),
            pltpu.VMEM((2 * rows, width), jnp.float32),
            pltpu.VMEM((2 * rows, width), bf),
            pltpu.VMEM((rows, width), bf),
            dma((9,)), dma((9,)),
            dma((36,)), dma((36,)),
            dma((9,)), dma((9,)),
            dma((12,)), dma((12,)),
            dma((8,)),
            dma((29,)), dma((29,)),
            dma((4,)), dma((7,)),
        ],
        compiler_params=pltpu.CompilerParams(
            collective_id=0, has_side_effects=True, vmem_limit_bytes=60 << 20
        ),
        name="attend",
    )(query_tokens, key_tokens, value_tokens, out_weight, lists)


def solution(mesh):
    placed = (
        P(("blk", "head"), None),
        P(("blk", "head"), None),
        P(("blk", "head"), None),
        P("head", None),
        P("blk", None),
    )
    return jax.shard_map(
        on_device, mesh=mesh, in_specs=placed, out_specs=P(("blk", "head"), None), check_vma=False
    )
```

```python
import functools
import math

import jax
import jax.numpy as jnp
from jax import lax
from jax.experimental import pallas as pl
from jax.experimental.pallas import tpu as pltpu
from jax.sharding import PartitionSpec as P

HD = 128
BLK = 128
HEADS_DEV = 3
NAMES = ("unit", "merge", "proj", "qsend", "qfwd", "w1r", "w1", "w2r", "xor", "xo")
MESH = pl.DeviceIdType.MESH
ABSENT = -(2.0**100)
SCALE = math.log2(math.e) / math.sqrt(HD)

OWN, M1, P1, M2, P2, MIR, TMP = range(7)
UP = {1: M1, 2: M2, 3: TMP, 4: MIR}
DOWN = {1: P1, 2: P2, 3: TMP, 4: MIR}
HOPS = [(kind, h, hop) for h in range(HEADS_DEV) for kind, n in (("A", 4), ("B", 2)) for hop in range(1, n + 1)]
JOBS = (
    "a2aV0", "a2aK0", "a2aK1", "a2aV1", "a2aV2", "zUB01", "zDA01", "a2aQ2", "zUA01", "zDB01", "a2aQ0",
    "zUA11", "zDB11", "a2aQ1", "zUB11", "zDA11", "a2aK2", "xo0", "w12", "w10", "qsend2", "zDA02", "zUB02",
    "qsend0", "qsend1", "zUA02", "zDB02", "zUA12", "zDB12", "qfwd2", "zUB12", "zDA12", "qfwd0", "w11",
    "zUA21", "zDA03", "qfwd1", "unit03", "zUA03", "zDA21", "unit02", "unit01", "zUB21", "zDB21", "xor0",
    "unit13", "w1r2", "zDA13", "zUA13", "unit12", "unit11", "zDA04", "zUA22", "zUA04", "zDA22", "zUB22",
    "zDB22", "w1r0", "zUA14", "zDA14", "w2r2", "zUA23", "w1r1", "unit00", "zDA23", "merge0", "w2r0",
    "unit22", "xor1", "xor2", "unit23", "unit10", "merge1", "w2r1", "proj0", "zUA24", "zDA24", "unit21",
    "proj1", "xor3", "unit20", "merge2", "final",
)


def kernel(q_hbm, k_hbm, v_hbm, w_hbm, kvb_ref, out_ref, *scratch):
    nh = HEADS_DEV
    kb, vb, qb_, os_, or_, wb, att, ab, km, vm = (scratch[i * nh : (i + 1) * nh] for i in range(10))
    (kvb_all, kvb_smem, pacc, pb, prec, a_send, a_recv, zs, zr, qs, qr, osem, orsem, misc, ws, wr, ts, tr) = scratch[10 * nh :]
    b = lax.axis_index("blk")
    g = lax.axis_index("head")
    z, r = lax.div(b, 4), lax.rem(b, 4)
    xl, c = lax.div(r, 2), lax.rem(r, 2)
    ghalf, glow = lax.div(g, 2), lax.rem(g, 2)
    plane = [(xl, c), (xl, 1 - c), (1 - xl, c), (1 - xl, 1 - c)]
    plane_r = [x * 2 + cc for x, cc in plane]
    plane_dev = [(z * 4 + rr, g) for rr in plane_r]
    xh, y = lax.div(g, 4), lax.rem(g, 4)
    xo_dev = (z * 4 + (1 - xl) * 2 + c, (1 - xh) * 4 + y)
    xh_dev = (b, (1 - xh) * 4 + y)
    zdev = {"U": (lax.rem(z + 1, 8) * 4 + r, g), "D": (lax.rem(z + 7, 8) * 4 + r, g)}

    def head_dev(d):
        return lax.rem(g + d, 8)

    barrier = pltpu.get_barrier_semaphore()
    for dev in plane_dev[1:] + list(zdev.values()) + [(b, head_dev(d)) for d in range(1, 8)] + [xo_dev]:
        pl.semaphore_signal(barrier, inc=1, device_id=dev, device_id_type=MESH)
    pl.semaphore_wait(barrier, 13)

    def wait_bytes(ref, sem):
        pltpu.make_async_copy(ref, ref, sem).wait()

    done = set()

    src = {"K": k_hbm, "V": v_hbm, "Q": q_hbm}

    def a2a_dst(x, h):
        if x == "Q":
            return qb_[h], r * 4
        return (kb if x == "K" else vb)[h], OWN * 4

    a2a_idx = {}
    for h in range(nh):
        for x in "KVQ":
            a2a_idx[x, h] = len(a2a_idx)

    def a2a_start(x, h):
        i = a2a_idx[x, h]
        buf, base = a2a_dst(x, h)
        dst = buf.at[base + ghalf, pl.ds(pl.multiple_of(glow * 64, 64), 64), :]

        def cols(dest):
            return src[x].at[:, pl.ds(pl.multiple_of(dest * (nh * HD) + h * HD, HD), HD)]

        pltpu.make_async_copy(cols(g), dst, a_recv.at[i]).start()

        def one(d, carry):
            dest = head_dev(d)
            pltpu.make_async_remote_copy(
                src_ref=cols(dest), dst_ref=dst, send_sem=a_send.at[i], recv_sem=a_recv.at[i],
                device_id=(b, dest), device_id_type=MESH,
            ).start()
            return carry

        lax.fori_loop(1, 8, one, 0)

    def a2a_wait(x, h):
        if ("a2a", x, h) in done:
            return
        done.add(("a2a", x, h))
        buf, base = a2a_dst(x, h)
        wait_bytes(buf.at[pl.ds(base, 4)], a_recv.at[a2a_idx[x, h]])

    kv_copies = []
    for i in range(1, 4):
        kv_copies.append(
            pltpu.make_async_remote_copy(
                src_ref=kvb_ref, dst_ref=kvb_all.at[r], send_sem=misc.at[2 * i], recv_sem=misc.at[2 * i + 1],
                device_id=plane_dev[i], device_id_type=MESH,
            )
        )
    kv_own = pltpu.make_async_copy(kvb_ref, kvb_all.at[r], misc.at[0])


    def tensor(direction, kind):
        return (kb, km) if (direction == "U") == (kind == "A") else (vb, vm)

    def slot_ref(bufs, h, slot):
        return bufs[0][h].at[pl.ds(slot * 4, 4)] if slot < MIR else bufs[1][h].at[pl.ds((slot - MIR) * 4, 4)]

    zname = {}

    def zcopy(direction, kind, h, hop):
        slots = UP if direction == "U" else DOWN
        bufs = tensor(direction, kind)
        s_src = OWN if hop == 1 else slots[hop - 1]
        s_dst = slots[hop]
        k = HOPS.index((kind, h, hop)) + (len(HOPS) if direction == "D" else 0)
        return pltpu.make_async_remote_copy(
            src_ref=slot_ref(bufs, h, s_src), dst_ref=slot_ref(bufs, h, s_dst),
            send_sem=zs.at[k], recv_sem=zr.at[k], device_id=zdev[direction], device_id_type=MESH,
        )

    def z_wait(*key):
        if key not in done:
            done.add(key)
            zcopy(*key).wait_recv()

    def z_step(direction, kind, h, hop):
        if hop == 1:
            is_k = (direction == "U") == (kind == "A")
            a2a_wait("K" if is_k else "V", h)
        else:
            z_wait(direction, kind, h, hop - 1)
        zcopy(direction, kind, h, hop).start()

    def q_copy(h, i):
        ref = qb_[h].at[pl.ds(plane_r[2 if i == 3 else 0] * 4, 4)]
        return pltpu.make_async_remote_copy(
            src_ref=ref, dst_ref=ref, send_sem=qs.at[h * 3 + i - 1], recv_sem=qr.at[h * 3 + i - 1],
            device_id=plane_dev[2 if i == 2 else 1], device_id_type=MESH,
        )

    def q_send(h):
        a2a_wait("Q", h)
        for i in (2, 1):
            q_copy(h, i).start()

    def q_fwd(h):
        q_wait(h, (2,))
        q_copy(h, 3).start()

    def q_wait(h, which=(1, 2, 3)):
        for i in which:
            if ("q", h, i) not in done:
                done.add(("q", h, i))
                wait_bytes(qb_[h].at[pl.ds(plane_r[i] * 4, 4)], qr.at[h * 3 + i - 1])

    def kvb_wait():
        if "kvb" in done:
            return
        done.add("kvb")
        kv_own.wait()
        for i in range(1, 4):
            kv_copies[i - 1].wait()
        cp = pltpu.make_async_copy(kvb_all, kvb_smem, misc.at[1])
        cp.start()
        cp.wait()

    lane = lax.broadcasted_iota(jnp.int32, (BLK, BLK), 1)
    ones = jnp.ones((BLK, HD), jnp.bfloat16)

    def o_copy(h, i):
        return pltpu.make_async_remote_copy(
            src_ref=os_[h].at[i], dst_ref=or_[h].at[i], send_sem=osem.at[h * 4 + i], recv_sem=orsem.at[h * 4 + i],
            device_id=plane_dev[i], device_id_type=MESH,
        )

    def unit(h, i):
        kvb_wait()
        q_wait(h)
        for x in "KV":
            a2a_wait(x, h)
        for kind, hh, hop in HOPS:
            if hh == h and hop in ((1, 2, 4) if i == 0 else (1, 2)):
                z_wait("U", kind, h, hop)
                z_wait("D", kind, h, hop)
        rq = plane_r[i]
        dl = r - rq
        gt = lax.div(dl + 3, 4)
        lt = lax.div(3 - dl, 4)
        eq = 1 - gt - lt
        picks = [
            (OWN, gt * (2 * dl) + lt * (1 - 2 * dl)),
            (M1, 9 - 2 * dl),
            (P1, 2 * dl + 8),
            (0 if i == 0 else M2 * gt + P2 * lt, gt * (17 - 2 * dl) + lt * (2 * dl + 16) + eq),
        ]

        def block(j, stats):
            q = qb_[h][rq * 4 + j]
            scores, vals = [], []
            for n, (slot, col) in enumerate(picks):
                keys, values = (km[h], vm[h]) if n == 3 and i == 0 else (kb[h], vb[h])
                e = kvb_smem[rq, j, col]
                idx = slot * 4 + jnp.bitwise_and(e, 3)
                bias = jnp.where(e >= 0, 0.0, ABSENT).astype(jnp.float32)
                s = lax.dot_general(q, keys[idx], (((1,), (1,)), ((), ())), preferred_element_type=jnp.float32)
                scores.append(s * SCALE + bias)
                vals.append(jnp.concatenate([values[idx], ones], axis=1))
            top = functools.reduce(jnp.maximum, scores)
            m = jnp.max(top, axis=1, keepdims=True).astype(jnp.bfloat16).astype(jnp.float32)
            ps = [jnp.exp2(s - m).astype(jnp.bfloat16) for s in scores]
            o = functools.reduce(
                jnp.add,
                [jnp.dot(p, v, preferred_element_type=jnp.float32) for p, v in zip(ps, vals)],
            )
            os_[h][i, j] = o[:, :HD].astype(jnp.bfloat16)
            l = o[:, HD:]
            l_hi = l.astype(jnp.bfloat16).astype(jnp.float32)
            stats = jnp.where(lane == j, m, stats)
            stats = jnp.where(lane == j + 4, l_hi, stats)
            return jnp.where(lane == j + 8, l - l_hi, stats)

        stats = lax.fori_loop(0, 4, block, jnp.zeros((BLK, BLK), jnp.float32), unroll=4)
        os_[h][i, 4] = stats.astype(jnp.bfloat16)
        if i:
            o_copy(h, i).start()

    def merge(h):
        for i in (1, 2, 3):
            o_copy(h, i).wait_recv()
        bufs = [os_[h].at[0]] + [or_[h].at[i] for i in (1, 2, 3)]
        stats = [bf[4].astype(jnp.float32) for bf in bufs]
        for j in range(4):
            ms = [s[:, j : j + 1] for s in stats]
            ls = [s[:, j + 4 : j + 5] + s[:, j + 8 : j + 9] for s in stats]
            top = functools.reduce(jnp.maximum, ms)
            ws = [jnp.exp2(m - top) for m in ms]
            inv = 1.0 / functools.reduce(jnp.add, [w * l for w, l in zip(ws, ls)])
            o = functools.reduce(
                jnp.add, [(w * inv) * bf[j].astype(jnp.float32) for w, bf in zip(ws, bufs)]
            )
            att[h][j * BLK : (j + 1) * BLK, :] = o.astype(jnp.bfloat16)
        att_copies(h)

    def att_copies(h):
        def rows(gg):
            return att[h].at[pl.ds(pl.multiple_of(gg * 64, 64), 64), :]

        if h < 2:
            col = pl.ds(pl.multiple_of(y * HD, HD), HD)
            for p in range(2):
                dst = ab[h].at[p, :, col]
                pltpu.make_async_copy(rows(p * 4 + y), dst, tr.at[h]).start()
                for d in (2, 1, 3):
                    yy = lax.rem(y + d, 4)
                    pltpu.make_async_remote_copy(
                        src_ref=rows(p * 4 + yy), dst_ref=dst, send_sem=ts.at[h], recv_sem=tr.at[h],
                        device_id=(b, xh * 4 + yy), device_id_type=MESH,
                    ).start()
        else:
            dst = ab[h].at[:, pl.ds(pl.multiple_of(g * HD, HD), HD)]
            pltpu.make_async_copy(rows(g), dst, tr.at[h]).start()
            for d in range(1, 8):
                gg = head_dev(d)
                pltpu.make_async_remote_copy(
                    src_ref=rows(gg), dst_ref=dst, send_sem=ts.at[h], recv_sem=tr.at[h],
                    device_id=(b, gg), device_id_type=MESH,
                ).start()

    half = w_hbm.shape[1] // 2
    wcol = pl.ds(pl.multiple_of(c * half, 128), half)
    ocol = pl.ds(pl.multiple_of((1 - c) * half, 128), half)
    ydev = {d: (b, xh * 4 + lax.rem(y + d, 4)) for d in (1, 2, 3)}

    def widx(h, d, other=False):
        base = 0 if h < 2 else (1 - xh if other else xh) * 4
        return base + lax.rem(y + d, 4)

    def remote(src_ref, dst_ref, i, dev):
        return pltpu.make_async_remote_copy(
            src_ref=src_ref, dst_ref=dst_ref, send_sem=ws.at[i], recv_sem=wr.at[i], device_id=dev, device_id_type=MESH
        )

    def w_hop1(h, d):
        return remote(
            w_hbm.at[h * HD : (h + 1) * HD, wcol], wb[h].at[widx(h, 0), :, wcol], h * 7 + (0 if d == 1 else 1), ydev[d]
        )

    def w_hop2(h, d):
        ref = wb[h].at[widx(h, 4 - d), pl.ds(0 if d == 1 else 64, 64), wcol]
        return remote(ref, ref, h * 7 + (2 if d == 1 else 3), ydev[d])

    def w_sib(h, d):
        ref = wb[h].at[widx(h, d), :, wcol]
        return remote(ref, ref, h * 7 + 3 + d, plane_dev[1])

    def x_piece(k):
        dst = wb[2].at[widx(2, k), :, wcol]
        return remote(w_hbm.at[2 * HD : 3 * HD, wcol] if k == 0 else dst, dst, 21 + k, xo_dev)

    def x_sib(k):
        ref = wb[2].at[widx(2, k, True), :, wcol]
        return remote(ref, ref, 25 + k, plane_dev[1])

    def w_own(h):
        return pltpu.make_async_copy(w_hbm.at[h * HD : (h + 1) * HD, :], wb[h].at[widx(h, 0)], tr.at[3 + h])

    wsends = []

    def go(cp):
        cp.start()
        wsends.append(cp)

    def w_ready(h):
        w_own(h).wait()
        for d in (1, 2, 3):
            wait_bytes(wb[h].at[widx(h, d), :, ocol], wr.at[h * 7 + 3 + d])
        if h == 2:
            for k in range(4):
                wait_bytes(wb[2].at[widx(2, k, True), :, ocol], wr.at[25 + k])

    step = 512

    def columns(t):
        return pl.ds(pl.multiple_of(t * step, step), step)

    def project(h):
        w_ready(h)
        wait_bytes(ab[h], tr.at[h])
        rows = ab[h][...].reshape(2 * 64, 4 * HD)

        def one(t, carry):
            col = columns(t)
            res = jnp.dot(rows, wb[h][:, :, col].reshape(4 * HD, step), preferred_element_type=jnp.float32)
            if h:
                res = res + pacc[:, col]
                pb[:, col] = res.astype(jnp.bfloat16)
            pacc[:, col] = res
            return carry

        lax.fori_loop(0, pacc.shape[1] // step, one, 0)
        if h:
            p_copy.start()

    p_copy = pltpu.make_async_remote_copy(
        src_ref=pb.at[pl.ds(pl.multiple_of((1 - xh) * 64, 64), 64), :], dst_ref=prec,
        send_sem=ts.at[3], recv_sem=tr.at[6], device_id=xh_dev, device_id_type=MESH,
    )

    def final():
        w_ready(2)
        wait_bytes(ab[2], tr.at[2])
        p_copy.wait_recv()
        rows = ab[2][...]

        def one(t, carry):
            col = columns(t)
            res = jnp.dot(rows, wb[2][:, :, col].reshape(8 * HD, step), preferred_element_type=jnp.float32)
            mine = pacc[pl.ds(pl.multiple_of(xh * 64, 64), 64), col]
            out_ref[:, col] = (res + mine + prec[:, col].astype(jnp.float32)).astype(jnp.bfloat16)
            return carry

        lax.fori_loop(0, pacc.shape[1] // step, one, 0)

    def job(text):
        if text[:3] == "a2a":
            a2a_start(text[3], int(text[4]))
            return
        if text[0] == "z":
            z_step(text[1], text[2], int(text[3]), int(text[4]))
            return
        if text == "final":
            final()
            return
        name = next(a for a in NAMES if text.startswith(a))
        v = [int(a) for a in text[len(name) :]]
        if name == "unit":
            unit(*v)
        elif name == "merge":
            merge(*v)
        elif name == "proj":
            project(*v)
        elif name == "qsend":
            q_send(*v)
        elif name == "qfwd":
            q_fwd(*v)
        elif name == "w1":
            go(w_hop1(v[0], 1))
            go(w_hop1(v[0], 3))
        elif name == "w1r":
            h = v[0]
            w_hop1(h, 1).wait_recv()
            w_hop1(h, 3).wait_recv()
            go(w_hop2(h, 1))
            go(w_hop2(h, 3))
            go(w_sib(h, 1))
            go(w_sib(h, 3))
            if h == 2:
                go(x_piece(1))
                go(x_piece(3))
        elif name == "w2r":
            h = v[0]
            w_hop2(h, 1).wait_recv()
            w_hop2(h, 3).wait_recv()
            go(w_sib(h, 2))
            if h == 2:
                go(x_piece(2))
        elif name == "xo":
            go(x_piece(0))
        elif name == "xor":
            k = (0, 1, 3, 2)[v[0]]
            x_piece(k).wait_recv()
            go(x_sib(k))

    kv_own.start()
    for cp in kv_copies:
        cp.start()
    for text in JOBS[:2]:
        job(text)
    for h in range(nh):
        w_own(h).start()
    for text in JOBS[2:]:
        job(text)

    for key in HOPS:
        for direction in "UD":
            zcopy(direction, *key).wait_send()
    for h in range(nh):
        for i in (1, 2, 3):
            q_copy(h, i).wait_send()
            o_copy(h, i).wait_send()
    for (x, h), i in a2a_idx.items():
        wait_bytes(src[x].at[:, pl.ds(0, 7 * HD)], a_send.at[i])
    for cp in wsends:
        cp.wait_send()
    wait_bytes(att[0].at[pl.ds(0, 6 * 64)], ts.at[0])
    wait_bytes(att[1].at[pl.ds(0, 6 * 64)], ts.at[1])
    wait_bytes(att[2].at[pl.ds(0, 7 * 64)], ts.at[2])
    p_copy.wait_send()


def on_device(query_tokens, key_tokens, value_tokens, out_weight, kv_blocks):
    nh = HEADS_DEV
    rows, width = query_tokens.shape
    any_spec = pl.BlockSpec(memory_space=pl.ANY)
    vm = pl.BlockSpec(memory_space=pltpu.VMEM)
    bf = jnp.bfloat16
    dma = pltpu.SemaphoreType.DMA
    return pl.pallas_call(
        kernel,
        out_shape=jax.ShapeDtypeStruct((rows, width), bf),
        in_specs=[any_spec, any_spec, any_spec, any_spec, vm],
        out_specs=vm,
        scratch_shapes=[pltpu.VMEM((20, BLK, HD), bf)] * (2 * nh)
        + [pltpu.VMEM((16, BLK, HD), bf)] * nh
        + [pltpu.VMEM((4, 5, BLK, HD), bf)] * (2 * nh)
        + [pltpu.VMEM((n, HD, width), bf) for n in (4, 4, 8)]
        + [pltpu.VMEM((8 * rows, HD), bf)] * nh
        + [pltpu.VMEM((2, rows, 4 * HD), bf)] * 2
        + [pltpu.VMEM((rows, 8 * HD), bf)]
        + [pltpu.VMEM((8, BLK, HD), bf)] * (2 * nh)
        + [
            pltpu.VMEM((4, *kv_blocks.shape), jnp.int32),
            pltpu.SMEM((4, *kv_blocks.shape), jnp.int32),
            pltpu.VMEM((2 * rows, width), jnp.float32),
            pltpu.VMEM((2 * rows, width), bf),
            pltpu.VMEM((rows, width), bf),
            dma((9,)), dma((9,)),
            dma((36,)), dma((36,)),
            dma((9,)), dma((9,)),
            dma((12,)), dma((12,)),
            dma((8,)),
            dma((29,)), dma((29,)),
            dma((4,)), dma((7,)),
        ],
        compiler_params=pltpu.CompilerParams(
            collective_id=0, has_side_effects=True, vmem_limit_bytes=60 << 20
        ),
        name="attend",
    )(query_tokens, key_tokens, value_tokens, out_weight, kv_blocks)


def solution(mesh):
    placed = (
        P(("blk", "head"), None),
        P(("blk", "head"), None),
        P(("blk", "head"), None),
        P("head", None),
        P("blk", None),
    )
    return jax.shard_map(
        on_device, mesh=mesh, in_specs=placed, out_specs=P(("blk", "head"), None), check_vma=False
    )
```

```python
import functools
import math

import jax
import jax.numpy as jnp
from jax import lax
from jax.experimental import pallas as pl
from jax.experimental.pallas import tpu as pltpu
from jax.sharding import PartitionSpec as P

HD = 128
BLK = 128
HEADS_DEV = 3
NAMES = ("unit", "merge", "proj", "qsend", "qfwd", "w1r", "w1", "w2r", "xor", "xo")
MESH = pl.DeviceIdType.MESH
ABSENT = -(2.0**100)
SCALE = math.log2(math.e) / math.sqrt(HD)

OWN, M1, P1, M2, P2, MIR, TMP = range(7)
UP = {1: M1, 2: M2, 3: TMP, 4: MIR}
DOWN = {1: P1, 2: P2, 3: TMP, 4: MIR}
HOPS = [(kind, h, hop) for h in range(HEADS_DEV) for kind, n in (("A", 4), ("B", 2)) for hop in range(1, n + 1)]
JOBS = (
    "a2aK0", "a2aV0", "a2aV1", "a2aK1", "a2aQ0", "zUA01", "zDB01", "a2aQ2", "zUB01", "zDA01", "a2aQ1",
    "zUB11", "zDA11", "a2aV2", "zUA11", "zDB11", "a2aK2", "w11", "w12", "xo0", "qsend0", "zUA02", "zDB02",
    "qsend2", "qsend1", "zUB02", "zDA02", "zUB21", "zDA21", "zDB21", "zUA21", "zDA12", "zUB12", "zDB12",
    "qfwd0", "zUA12", "qfwd2", "w10", "zUA03", "qfwd1", "zDA03", "unit02", "unit01", "unit03", "zDA22",
    "zUB22", "xor0", "zUA22", "zDB22", "w1r1", "w1r2", "zDA13", "zUA13", "unit11", "unit13", "unit12",
    "zDA04", "zUA04", "zDA23", "zUA23", "unit22", "unit23", "w1r0", "zUA14", "zDA14", "unit21", "w2r1",
    "w2r2", "unit00", "merge0", "xor1", "xor2", "zUA24", "zDA24", "w2r0", "unit10", "merge1", "proj0",
    "unit20", "merge2", "xor3", "proj1", "proj2", "final",
)


def kernel(q_hbm, k_hbm, v_hbm, w_hbm, kvb_ref, out_ref, *scratch):
    nh = HEADS_DEV
    kb, vb, qb_, os_, or_, wb, att, ab, km, vm = (scratch[i * nh : (i + 1) * nh] for i in range(10))
    (kvb_all, kvb_smem, pacc, pb, prec, obuf, a_send, a_recv, zs, zr, qs, qr, osem, orsem, misc, ws, wr, ts, tr) = scratch[10 * nh :]
    b = lax.axis_index("blk")
    g = lax.axis_index("head")
    z, r = lax.div(b, 4), lax.rem(b, 4)
    xl, c = lax.div(r, 2), lax.rem(r, 2)
    ghalf, glow = lax.div(g, 2), lax.rem(g, 2)
    plane = [(xl, c), (xl, 1 - c), (1 - xl, c), (1 - xl, 1 - c)]
    plane_r = [x * 2 + cc for x, cc in plane]
    plane_dev = [(z * 4 + rr, g) for rr in plane_r]
    xh, y = lax.div(g, 4), lax.rem(g, 4)
    xo_dev = (z * 4 + (1 - xl) * 2 + c, (1 - xh) * 4 + y)
    xh_dev = (b, (1 - xh) * 4 + y)
    zdev = {"U": (lax.rem(z + 1, 8) * 4 + r, g), "D": (lax.rem(z + 7, 8) * 4 + r, g)}

    def head_dev(d):
        return lax.rem(g + d, 8)

    barrier = pltpu.get_barrier_semaphore()
    for dev in plane_dev[1:] + list(zdev.values()) + [(b, head_dev(d)) for d in range(1, 8)] + [xo_dev]:
        pl.semaphore_signal(barrier, inc=1, device_id=dev, device_id_type=MESH)
    pl.semaphore_wait(barrier, 13)

    def wait_bytes(ref, sem):
        pltpu.make_async_copy(ref, ref, sem).wait()

    done = set()

    src = {"K": k_hbm, "V": v_hbm, "Q": q_hbm}

    def a2a_dst(x, h):
        if x == "Q":
            return qb_[h], r * 4
        return (kb if x == "K" else vb)[h], OWN * 4

    a2a_idx = {}
    for h in range(nh):
        for x in "KVQ":
            a2a_idx[x, h] = len(a2a_idx)

    def a2a_start(x, h):
        i = a2a_idx[x, h]
        buf, base = a2a_dst(x, h)
        dst = buf.at[base + ghalf, pl.ds(pl.multiple_of(glow * 64, 64), 64), :]

        def cols(dest):
            return src[x].at[:, pl.ds(pl.multiple_of(dest * (nh * HD) + h * HD, HD), HD)]

        pltpu.make_async_copy(cols(g), dst, a_recv.at[i]).start()

        def one(d, carry):
            dest = head_dev(d)
            pltpu.make_async_remote_copy(
                src_ref=cols(dest), dst_ref=dst, send_sem=a_send.at[i], recv_sem=a_recv.at[i],
                device_id=(b, dest), device_id_type=MESH,
            ).start()
            return carry

        lax.fori_loop(1, 8, one, 0)

    def a2a_wait(x, h):
        if ("a2a", x, h) in done:
            return
        done.add(("a2a", x, h))
        buf, base = a2a_dst(x, h)
        wait_bytes(buf.at[pl.ds(base, 4)], a_recv.at[a2a_idx[x, h]])

    kv_copies = []
    for i in range(1, 4):
        kv_copies.append(
            pltpu.make_async_remote_copy(
                src_ref=kvb_ref, dst_ref=kvb_all.at[r], send_sem=misc.at[2 * i], recv_sem=misc.at[2 * i + 1],
                device_id=plane_dev[i], device_id_type=MESH,
            )
        )
    kv_own = pltpu.make_async_copy(kvb_ref, kvb_all.at[r], misc.at[0])


    def tensor(direction, kind):
        return (kb, km) if (direction == "U") == (kind == "A") else (vb, vm)

    def slot_ref(bufs, h, slot):
        return bufs[0][h].at[pl.ds(slot * 4, 4)] if slot < MIR else bufs[1][h].at[pl.ds((slot - MIR) * 4, 4)]

    zname = {}

    def zcopy(direction, kind, h, hop):
        slots = UP if direction == "U" else DOWN
        bufs = tensor(direction, kind)
        s_src = OWN if hop == 1 else slots[hop - 1]
        s_dst = slots[hop]
        k = HOPS.index((kind, h, hop)) + (len(HOPS) if direction == "D" else 0)
        return pltpu.make_async_remote_copy(
            src_ref=slot_ref(bufs, h, s_src), dst_ref=slot_ref(bufs, h, s_dst),
            send_sem=zs.at[k], recv_sem=zr.at[k], device_id=zdev[direction], device_id_type=MESH,
        )

    def z_wait(*key):
        if key not in done:
            done.add(key)
            zcopy(*key).wait_recv()

    def z_step(direction, kind, h, hop):
        if hop == 1:
            is_k = (direction == "U") == (kind == "A")
            a2a_wait("K" if is_k else "V", h)
        else:
            z_wait(direction, kind, h, hop - 1)
        zcopy(direction, kind, h, hop).start()

    def q_copy(h, i):
        ref = qb_[h].at[pl.ds(plane_r[2 if i == 3 else 0] * 4, 4)]
        return pltpu.make_async_remote_copy(
            src_ref=ref, dst_ref=ref, send_sem=qs.at[h * 3 + i - 1], recv_sem=qr.at[h * 3 + i - 1],
            device_id=plane_dev[2 if i == 2 else 1], device_id_type=MESH,
        )

    def q_send(h):
        a2a_wait("Q", h)
        for i in (2, 1):
            q_copy(h, i).start()

    def q_fwd(h):
        q_wait(h, (2,))
        q_copy(h, 3).start()

    def q_wait(h, which=(1, 2, 3)):
        for i in which:
            if ("q", h, i) not in done:
                done.add(("q", h, i))
                wait_bytes(qb_[h].at[pl.ds(plane_r[i] * 4, 4)], qr.at[h * 3 + i - 1])

    def kvb_wait():
        if "kvb" in done:
            return
        done.add("kvb")
        kv_own.wait()
        for i in range(1, 4):
            kv_copies[i - 1].wait()
        cp = pltpu.make_async_copy(kvb_all, kvb_smem, misc.at[1])
        cp.start()
        cp.wait()

    lane = lax.broadcasted_iota(jnp.int32, (BLK, BLK), 1)
    ones = jnp.ones((BLK, HD), jnp.bfloat16)

    def o_copy(h, i):
        return pltpu.make_async_remote_copy(
            src_ref=os_[h].at[i], dst_ref=or_[h].at[i], send_sem=osem.at[h * 4 + i], recv_sem=orsem.at[h * 4 + i],
            device_id=plane_dev[i], device_id_type=MESH,
        )

    def unit(h, i):
        kvb_wait()
        q_wait(h)
        for x in "KV":
            a2a_wait(x, h)
        for kind, hh, hop in HOPS:
            if hh == h and hop in ((1, 2, 4) if i == 0 else (1, 2)):
                z_wait("U", kind, h, hop)
                z_wait("D", kind, h, hop)
        rq = plane_r[i]
        dl = r - rq
        gt = lax.div(dl + 3, 4)
        lt = lax.div(3 - dl, 4)
        eq = 1 - gt - lt
        picks = [
            (OWN, gt * (2 * dl) + lt * (1 - 2 * dl)),
            (M1, 9 - 2 * dl),
            (P1, 2 * dl + 8),
            (0 if i == 0 else M2 * gt + P2 * lt, gt * (17 - 2 * dl) + lt * (2 * dl + 16) + eq),
        ]

        def block(j, stats):
            q = qb_[h][rq * 4 + j]
            scores, vals = [], []
            for n, (slot, col) in enumerate(picks):
                keys, values = (km[h], vm[h]) if n == 3 and i == 0 else (kb[h], vb[h])
                e = kvb_smem[rq, j, col]
                idx = slot * 4 + jnp.bitwise_and(e, 3)
                bias = jnp.where(e >= 0, 0.0, ABSENT).astype(jnp.float32)
                s = lax.dot_general(q, keys[idx], (((1,), (1,)), ((), ())), preferred_element_type=jnp.float32)
                scores.append(s * SCALE + bias)
                vals.append(jnp.concatenate([values[idx], ones], axis=1))
            top = functools.reduce(jnp.maximum, scores)
            m = jnp.max(top, axis=1, keepdims=True).astype(jnp.bfloat16).astype(jnp.float32)
            ps = [jnp.exp2(s - m).astype(jnp.bfloat16) for s in scores]
            o = functools.reduce(
                jnp.add,
                [jnp.dot(p, v, preferred_element_type=jnp.float32) for p, v in zip(ps, vals)],
            )
            os_[h][i, j] = o[:, :HD].astype(jnp.bfloat16)
            l = o[:, HD:]
            l_hi = l.astype(jnp.bfloat16).astype(jnp.float32)
            stats = jnp.where(lane == j, m, stats)
            stats = jnp.where(lane == j + 4, l_hi, stats)
            return jnp.where(lane == j + 8, l - l_hi, stats)

        stats = lax.fori_loop(0, 4, block, jnp.zeros((BLK, BLK), jnp.float32), unroll=4)
        os_[h][i, 4] = stats.astype(jnp.bfloat16)
        if i:
            o_copy(h, i).start()

    def merge(h):
        for i in (1, 2, 3):
            o_copy(h, i).wait_recv()
        bufs = [os_[h].at[0]] + [or_[h].at[i] for i in (1, 2, 3)]
        stats = [bf[4].astype(jnp.float32) for bf in bufs]
        for j in range(4):
            ms = [s[:, j : j + 1] for s in stats]
            ls = [s[:, j + 4 : j + 5] + s[:, j + 8 : j + 9] for s in stats]
            top = functools.reduce(jnp.maximum, ms)
            ws = [jnp.exp2(m - top) for m in ms]
            inv = 1.0 / functools.reduce(jnp.add, [w * l for w, l in zip(ws, ls)])
            o = functools.reduce(
                jnp.add, [(w * inv) * bf[j].astype(jnp.float32) for w, bf in zip(ws, bufs)]
            )
            att[h][j * BLK : (j + 1) * BLK, :] = o.astype(jnp.bfloat16)
        att_copies(h)

    def att_copies(h):
        def rows(gg):
            return att[h].at[pl.ds(pl.multiple_of(gg * 64, 64), 64), :]

        if h < 2:
            col = pl.ds(pl.multiple_of(y * HD, HD), HD)
            for p in range(2):
                dst = ab[h].at[p, :, col]
                pltpu.make_async_copy(rows(p * 4 + y), dst, tr.at[h]).start()
                for d in (2, 1, 3):
                    yy = lax.rem(y + d, 4)
                    pltpu.make_async_remote_copy(
                        src_ref=rows(p * 4 + yy), dst_ref=dst, send_sem=ts.at[h], recv_sem=tr.at[h],
                        device_id=(b, xh * 4 + yy), device_id_type=MESH,
                    ).start()
        else:
            dst = ab[h].at[:, pl.ds(pl.multiple_of(g * HD, HD), HD)]
            pltpu.make_async_copy(rows(g), dst, tr.at[h]).start()
            for d in range(1, 8):
                gg = head_dev(d)
                pltpu.make_async_remote_copy(
                    src_ref=rows(gg), dst_ref=dst, send_sem=ts.at[h], recv_sem=tr.at[h],
                    device_id=(b, gg), device_id_type=MESH,
                ).start()

    half = w_hbm.shape[1] // 2
    wcol = pl.ds(pl.multiple_of(c * half, 128), half)
    ocol = pl.ds(pl.multiple_of((1 - c) * half, 128), half)
    ydev = {d: (b, xh * 4 + lax.rem(y + d, 4)) for d in (1, 2, 3)}

    def widx(h, d, other=False):
        base = 0 if h < 2 else (1 - xh if other else xh) * 4
        return base + lax.rem(y + d, 4)

    def remote(src_ref, dst_ref, i, dev):
        return pltpu.make_async_remote_copy(
            src_ref=src_ref, dst_ref=dst_ref, send_sem=ws.at[i], recv_sem=wr.at[i], device_id=dev, device_id_type=MESH
        )

    def w_hop1(h, d):
        return remote(
            w_hbm.at[h * HD : (h + 1) * HD, wcol], wb[h].at[widx(h, 0), :, wcol], h * 7 + (0 if d == 1 else 1), ydev[d]
        )

    def w_hop2(h, d):
        ref = wb[h].at[widx(h, 4 - d), pl.ds(0 if d == 1 else 64, 64), wcol]
        return remote(ref, ref, h * 7 + (2 if d == 1 else 3), ydev[d])

    def w_sib(h, d):
        ref = wb[h].at[widx(h, d), :, wcol]
        return remote(ref, ref, h * 7 + 3 + d, plane_dev[1])

    def x_piece(k):
        dst = wb[2].at[widx(2, k), :, wcol]
        return remote(w_hbm.at[2 * HD : 3 * HD, wcol] if k == 0 else dst, dst, 21 + k, xo_dev)

    def x_sib(k):
        ref = wb[2].at[widx(2, k, True), :, wcol]
        return remote(ref, ref, 25 + k, plane_dev[1])

    def w_own(h):
        return pltpu.make_async_copy(w_hbm.at[h * HD : (h + 1) * HD, :], wb[h].at[widx(h, 0)], tr.at[3 + h])

    wsends = []

    def go(cp):
        cp.start()
        wsends.append(cp)

    def w_ready(h):
        w_own(h).wait()
        for d in (1, 2, 3):
            wait_bytes(wb[h].at[widx(h, d), :, ocol], wr.at[h * 7 + 3 + d])
        if h == 2:
            for k in range(4):
                wait_bytes(wb[2].at[widx(2, k, True), :, ocol], wr.at[25 + k])

    step = 768

    def columns(t):
        return pl.ds(pl.multiple_of(t * step, step), step)

    def project(k):
        h = min(k, 1)
        if k < 2:
            w_ready(h)
            wait_bytes(ab[h], tr.at[h])
        rows = ab[h][...].reshape(2 * 64, 4 * HD)
        n = pacc.shape[1] // step

        def one(t, carry):
            col = columns(t)
            res = jnp.dot(rows, wb[h][:, :, col].reshape(4 * HD, step), preferred_element_type=jnp.float32)
            if h:
                res = res + pacc[:, col]
                pb[:, col] = res.astype(jnp.bfloat16)
            pacc[:, col] = res
            return carry

        lax.fori_loop(*((0, n), (0, n // 2), (n // 2, n))[k], one, 0)
        if h:
            p_copy(k - 1).start()

    def p_copy(k):
        n = pb.shape[1] // 2
        return pltpu.make_async_remote_copy(
            src_ref=pb.at[pl.ds(pl.multiple_of((1 - xh) * 64, 64), 64), k * n : (k + 1) * n],
            dst_ref=prec.at[:, k * n : (k + 1) * n],
            send_sem=ts.at[3 + k], recv_sem=tr.at[6 + k], device_id=xh_dev, device_id_type=MESH,
        )

    def out_copy(t):
        return pltpu.make_async_copy(obuf.at[:, columns(t)], out_ref.at[:, columns(t)], ts.at[5 + t])

    def final():
        w_ready(2)
        wait_bytes(ab[2], tr.at[2])
        rows = ab[2][...]
        n = pacc.shape[1] // step
        for t in range(n):
            if t % (n // 2) == 0:
                p_copy(t // (n // 2)).wait_recv()
            col = slice(t * step, (t + 1) * step)
            res = jnp.dot(rows, wb[2][:, :, col].reshape(8 * HD, step), preferred_element_type=jnp.float32)
            mine = pacc[pl.ds(pl.multiple_of(xh * 64, 64), 64), col]
            obuf[:, col] = (res + mine + prec[:, col].astype(jnp.float32)).astype(jnp.bfloat16)
            out_copy(t).start()

    def job(text):
        if text[:3] == "a2a":
            a2a_start(text[3], int(text[4]))
            return
        if text[0] == "z":
            z_step(text[1], text[2], int(text[3]), int(text[4]))
            return
        if text == "final":
            final()
            return
        name = next(a for a in NAMES if text.startswith(a))
        v = [int(a) for a in text[len(name) :]]
        if name == "unit":
            unit(*v)
        elif name == "merge":
            merge(*v)
        elif name == "proj":
            project(*v)
        elif name == "qsend":
            q_send(*v)
        elif name == "qfwd":
            q_fwd(*v)
        elif name == "w1":
            go(w_hop1(v[0], 1))
            go(w_hop1(v[0], 3))
        elif name == "w1r":
            h = v[0]
            w_hop1(h, 1).wait_recv()
            w_hop1(h, 3).wait_recv()
            go(w_hop2(h, 1))
            go(w_hop2(h, 3))
            go(w_sib(h, 1))
            go(w_sib(h, 3))
            if h == 2:
                go(x_piece(1))
                go(x_piece(3))
        elif name == "w2r":
            h = v[0]
            w_hop2(h, 1).wait_recv()
            w_hop2(h, 3).wait_recv()
            go(w_sib(h, 2))
            if h == 2:
                go(x_piece(2))
        elif name == "xo":
            go(x_piece(0))
        elif name == "xor":
            k = (0, 1, 3, 2)[v[0]]
            x_piece(k).wait_recv()
            go(x_sib(k))

    kv_own.start()
    for cp in kv_copies:
        cp.start()
    for text in JOBS[:2]:
        job(text)
    for h in range(nh):
        w_own(h).start()
    for text in JOBS[2:]:
        job(text)

    for key in HOPS:
        for direction in "UD":
            zcopy(direction, *key).wait_send()
    for h in range(nh):
        for i in (1, 2, 3):
            q_copy(h, i).wait_send()
            o_copy(h, i).wait_send()
    for (x, h), i in a2a_idx.items():
        wait_bytes(src[x].at[:, pl.ds(0, 7 * HD)], a_send.at[i])
    for cp in wsends:
        cp.wait_send()
    wait_bytes(att[0].at[pl.ds(0, 6 * 64)], ts.at[0])
    wait_bytes(att[1].at[pl.ds(0, 6 * 64)], ts.at[1])
    wait_bytes(att[2].at[pl.ds(0, 7 * 64)], ts.at[2])
    for k in range(2):
        p_copy(k).wait_send()
    for t in range(pacc.shape[1] // step):
        out_copy(t).wait()


def on_device(query_tokens, key_tokens, value_tokens, out_weight, kv_blocks):
    nh = HEADS_DEV
    rows, width = query_tokens.shape
    any_spec = pl.BlockSpec(memory_space=pl.ANY)
    vm = pl.BlockSpec(memory_space=pltpu.VMEM)
    bf = jnp.bfloat16
    dma = pltpu.SemaphoreType.DMA
    return pl.pallas_call(
        kernel,
        out_shape=jax.ShapeDtypeStruct((rows, width), bf),
        in_specs=[any_spec, any_spec, any_spec, any_spec, vm],
        out_specs=any_spec,
        scratch_shapes=[pltpu.VMEM((20, BLK, HD), bf)] * (2 * nh)
        + [pltpu.VMEM((16, BLK, HD), bf)] * nh
        + [pltpu.VMEM((4, 5, BLK, HD), bf)] * (2 * nh)
        + [pltpu.VMEM((n, HD, width), bf) for n in (4, 4, 8)]
        + [pltpu.VMEM((8 * rows, HD), bf)] * nh
        + [pltpu.VMEM((2, rows, 4 * HD), bf)] * 2
        + [pltpu.VMEM((rows, 8 * HD), bf)]
        + [pltpu.VMEM((8, BLK, HD), bf)] * (2 * nh)
        + [
            pltpu.VMEM((4, *kv_blocks.shape), jnp.int32),
            pltpu.SMEM((4, *kv_blocks.shape), jnp.int32),
            pltpu.VMEM((2 * rows, width), jnp.float32),
            pltpu.VMEM((2 * rows, width), bf),
            pltpu.VMEM((rows, width), bf),
            pltpu.VMEM((rows, width), bf),
            dma((9,)), dma((9,)),
            dma((36,)), dma((36,)),
            dma((9,)), dma((9,)),
            dma((12,)), dma((12,)),
            dma((8,)),
            dma((29,)), dma((29,)),
            dma((9,)), dma((8,)),
        ],
        compiler_params=pltpu.CompilerParams(
            collective_id=0, has_side_effects=True, vmem_limit_bytes=60 << 20
        ),
        name="attend",
    )(query_tokens, key_tokens, value_tokens, out_weight, kv_blocks)


def solution(mesh):
    placed = (
        P(("blk", "head"), None),
        P(("blk", "head"), None),
        P(("blk", "head"), None),
        P("head", None),
        P("blk", None),
    )
    return jax.shard_map(
        on_device, mesh=mesh, in_specs=placed, out_specs=P(("blk", "head"), None), check_vma=False
    )
```

```python
import functools
import math

import jax
import jax.numpy as jnp
from jax import lax
from jax.experimental import pallas as pl
from jax.experimental.pallas import tpu as pltpu
from jax.sharding import PartitionSpec as P

HD = 128
BLK = 128
HEADS_DEV = 3
NAMES = ("unit", "merge", "proj", "qsend", "qfwd", "w1r", "w1", "w2r", "xor", "xo")
MESH = pl.DeviceIdType.MESH
ABSENT = -(2.0**100)
SCALE = math.log2(math.e) / math.sqrt(HD)

OWN, M1, P1, M2, P2, MIR, TMP = range(7)
UP = {1: M1, 2: M2, 3: TMP, 4: MIR}
DOWN = {1: P1, 2: P2, 3: TMP, 4: MIR}
HOPS = [(kind, h, hop) for h in range(HEADS_DEV) for kind, n in (("A", 4), ("B", 2)) for hop in range(1, n + 1)]
JOBS = (
    "a2aK0", "a2aK1", "a2aV0", "a2aV1", "a2aK2", "a2aQ2", "a2aQ1", "a2aQ0", "a2aV2", "w12", "xo0", "w10",
    "w11", "zUA01", "zDB01", "zUA11", "zDB11", "zUB01", "zDA01", "zUB11", "zDA11", "zUA21", "zDB21", "zUA02",
    "qsend2", "zDB02", "qsend1", "zUA12", "qsend0", "zDB12", "zUB21", "zUB02", "zDA21", "qfwd2", "zUB12",
    "zDA02", "qfwd1", "zUA22", "zDB22", "xor0", "qfwd0", "zUA03", "zDA12", "zUA13", "zDA22", "w1r2", "zUB22",
    "w1r0", "unit03", "unit02", "unit01", "zDA03", "zUA23", "zDA13", "unit13", "unit11", "zDA23", "zUA04",
    "w2r2", "unit12", "zUA14", "zDA04", "w1r1", "zDA14", "unit22", "w2r0", "unit21", "xor1", "unit23",
    "zUA24", "xor2", "zDA24", "unit00", "w2r1", "merge0", "unit10", "merge1", "unit20", "merge2", "xor3",
    "proj0", "proj1", "proj2", "fin", "final",
)


def kernel(q_hbm, k_hbm, v_hbm, w_hbm, kvb_ref, out_ref, *scratch):
    nh = HEADS_DEV
    kb, vb, qb_, os_, or_, wb, att, ab, km, vm = (scratch[i * nh : (i + 1) * nh] for i in range(10))
    (kvb_all, kvb_smem, pacc, pb, prec, obuf, total, a_send, a_recv, zs, zr, qs, qr, osem, orsem, misc, ws, wr, ts, tr) = scratch[10 * nh :]
    b = lax.axis_index("blk")
    g = lax.axis_index("head")
    z, r = lax.div(b, 4), lax.rem(b, 4)
    xl, c = lax.div(r, 2), lax.rem(r, 2)
    ghalf, glow = lax.div(g, 2), lax.rem(g, 2)
    plane = [(xl, c), (xl, 1 - c), (1 - xl, c), (1 - xl, 1 - c)]
    plane_r = [x * 2 + cc for x, cc in plane]
    plane_dev = [(z * 4 + rr, g) for rr in plane_r]
    xh, y = lax.div(g, 4), lax.rem(g, 4)
    xo_dev = (z * 4 + (1 - xl) * 2 + c, (1 - xh) * 4 + y)
    xh_dev = (b, (1 - xh) * 4 + y)
    zdev = {"U": (lax.rem(z + 1, 8) * 4 + r, g), "D": (lax.rem(z + 7, 8) * 4 + r, g)}

    def head_dev(d):
        return lax.rem(g + d, 8)

    barrier = pltpu.get_barrier_semaphore()
    for dev in plane_dev[1:] + list(zdev.values()) + [(b, head_dev(d)) for d in range(1, 8)] + [xo_dev]:
        pl.semaphore_signal(barrier, inc=1, device_id=dev, device_id_type=MESH)
    pl.semaphore_wait(barrier, 13)

    def wait_bytes(ref, sem):
        pltpu.make_async_copy(ref, ref, sem).wait()

    done = set()

    src = {"K": k_hbm, "V": v_hbm, "Q": q_hbm}

    def a2a_dst(x, h):
        if x == "Q":
            return qb_[h], r * 4
        return (kb if x == "K" else vb)[h], OWN * 4

    a2a_idx = {}
    for h in range(nh):
        for x in "KVQ":
            a2a_idx[x, h] = len(a2a_idx)

    def a2a_start(x, h):
        i = a2a_idx[x, h]
        buf, base = a2a_dst(x, h)
        dst = buf.at[base + ghalf, pl.ds(pl.multiple_of(glow * 64, 64), 64), :]

        def cols(dest):
            return src[x].at[:, pl.ds(pl.multiple_of(dest * (nh * HD) + h * HD, HD), HD)]

        pltpu.make_async_copy(cols(g), dst, a_recv.at[i]).start()

        def one(d, carry):
            dest = head_dev(d)
            pltpu.make_async_remote_copy(
                src_ref=cols(dest), dst_ref=dst, send_sem=a_send.at[i], recv_sem=a_recv.at[i],
                device_id=(b, dest), device_id_type=MESH,
            ).start()
            return carry

        lax.fori_loop(1, 8, one, 0)

    def a2a_wait(x, h):
        if ("a2a", x, h) in done:
            return
        done.add(("a2a", x, h))
        buf, base = a2a_dst(x, h)
        wait_bytes(buf.at[pl.ds(base, 4)], a_recv.at[a2a_idx[x, h]])

    kv_copies = []
    for i in range(1, 4):
        kv_copies.append(
            pltpu.make_async_remote_copy(
                src_ref=kvb_ref, dst_ref=kvb_all.at[r], send_sem=misc.at[2 * i], recv_sem=misc.at[2 * i + 1],
                device_id=plane_dev[i], device_id_type=MESH,
            )
        )
    kv_own = pltpu.make_async_copy(kvb_ref, kvb_all.at[r], misc.at[0])


    def tensor(direction, kind):
        return (kb, km) if (direction == "U") == (kind == "A") else (vb, vm)

    def slot_ref(bufs, h, slot):
        return bufs[0][h].at[pl.ds(slot * 4, 4)] if slot < MIR else bufs[1][h].at[pl.ds((slot - MIR) * 4, 4)]

    zname = {}

    def zcopy(direction, kind, h, hop):
        slots = UP if direction == "U" else DOWN
        bufs = tensor(direction, kind)
        s_src = OWN if hop == 1 else slots[hop - 1]
        s_dst = slots[hop]
        k = HOPS.index((kind, h, hop)) + (len(HOPS) if direction == "D" else 0)
        return pltpu.make_async_remote_copy(
            src_ref=slot_ref(bufs, h, s_src), dst_ref=slot_ref(bufs, h, s_dst),
            send_sem=zs.at[k], recv_sem=zr.at[k], device_id=zdev[direction], device_id_type=MESH,
        )

    def z_wait(*key):
        if key not in done:
            done.add(key)
            zcopy(*key).wait_recv()

    def z_step(direction, kind, h, hop):
        if hop == 1:
            is_k = (direction == "U") == (kind == "A")
            a2a_wait("K" if is_k else "V", h)
        else:
            z_wait(direction, kind, h, hop - 1)
        zcopy(direction, kind, h, hop).start()

    def q_copy(h, i):
        ref = qb_[h].at[pl.ds(plane_r[2 if i == 3 else 0] * 4, 4)]
        return pltpu.make_async_remote_copy(
            src_ref=ref, dst_ref=ref, send_sem=qs.at[h * 3 + i - 1], recv_sem=qr.at[h * 3 + i - 1],
            device_id=plane_dev[2 if i == 2 else 1], device_id_type=MESH,
        )

    def q_send(h):
        a2a_wait("Q", h)
        for i in (2, 1):
            q_copy(h, i).start()

    def q_fwd(h):
        q_wait(h, (2,))
        q_copy(h, 3).start()

    def q_wait(h, which=(1, 2, 3)):
        for i in which:
            if ("q", h, i) not in done:
                done.add(("q", h, i))
                wait_bytes(qb_[h].at[pl.ds(plane_r[i] * 4, 4)], qr.at[h * 3 + i - 1])

    def kvb_wait():
        if "kvb" in done:
            return
        done.add("kvb")
        kv_own.wait()
        for i in range(1, 4):
            kv_copies[i - 1].wait()
        cp = pltpu.make_async_copy(kvb_all, kvb_smem, misc.at[1])
        cp.start()
        cp.wait()

    lane = lax.broadcasted_iota(jnp.int32, (BLK, BLK), 1)
    ones = jnp.ones((BLK, HD), jnp.bfloat16)

    def o_copy(h, i):
        return pltpu.make_async_remote_copy(
            src_ref=os_[h].at[i], dst_ref=or_[h].at[i], send_sem=osem.at[h * 4 + i], recv_sem=orsem.at[h * 4 + i],
            device_id=plane_dev[i], device_id_type=MESH,
        )

    def unit(h, i):
        kvb_wait()
        q_wait(h)
        for x in "KV":
            a2a_wait(x, h)
        for kind, hh, hop in HOPS:
            if hh == h and hop in ((1, 2, 4) if i == 0 else (1, 2)):
                z_wait("U", kind, h, hop)
                z_wait("D", kind, h, hop)
        rq = plane_r[i]
        dl = r - rq
        gt = lax.div(dl + 3, 4)
        lt = lax.div(3 - dl, 4)
        eq = 1 - gt - lt
        picks = [
            (OWN, gt * (2 * dl) + lt * (1 - 2 * dl)),
            (M1, 9 - 2 * dl),
            (P1, 2 * dl + 8),
            (0 if i == 0 else M2 * gt + P2 * lt, gt * (17 - 2 * dl) + lt * (2 * dl + 16) + eq),
        ]

        def block(j, stats):
            q = qb_[h][rq * 4 + j]
            scores, vals = [], []
            for n, (slot, col) in enumerate(picks):
                keys, values = (km[h], vm[h]) if n == 3 and i == 0 else (kb[h], vb[h])
                e = kvb_smem[rq, j, col]
                idx = slot * 4 + jnp.bitwise_and(e, 3)
                bias = jnp.where(e >= 0, 0.0, ABSENT).astype(jnp.float32)
                s = lax.dot_general(q, keys[idx], (((1,), (1,)), ((), ())), preferred_element_type=jnp.float32)
                scores.append(s * SCALE + bias)
                vals.append(jnp.concatenate([values[idx], ones], axis=1))
            top = functools.reduce(jnp.maximum, scores)
            m = jnp.max(top, axis=1, keepdims=True).astype(jnp.bfloat16).astype(jnp.float32)
            ps = [jnp.exp2(s - m).astype(jnp.bfloat16) for s in scores]
            o = functools.reduce(
                jnp.add,
                [jnp.dot(p, v, preferred_element_type=jnp.float32) for p, v in zip(ps, vals)],
            )
            os_[h][i, j] = o[:, :HD].astype(jnp.bfloat16)
            l = o[:, HD:]
            l_hi = l.astype(jnp.bfloat16).astype(jnp.float32)
            stats = jnp.where(lane == j, m, stats)
            stats = jnp.where(lane == j + 4, l_hi, stats)
            return jnp.where(lane == j + 8, l - l_hi, stats)

        stats = lax.fori_loop(0, 4, block, jnp.zeros((BLK, BLK), jnp.float32), unroll=4)
        os_[h][i, 4] = stats.astype(jnp.bfloat16)
        if i:
            o_copy(h, i).start()

    def merge(h):
        for i in (1, 2, 3):
            o_copy(h, i).wait_recv()
        bufs = [os_[h].at[0]] + [or_[h].at[i] for i in (1, 2, 3)]
        stats = [bf[4].astype(jnp.float32) for bf in bufs]
        for j in range(4):
            ms = [s[:, j : j + 1] for s in stats]
            ls = [s[:, j + 4 : j + 5] + s[:, j + 8 : j + 9] for s in stats]
            top = functools.reduce(jnp.maximum, ms)
            ws = [jnp.exp2(m - top) for m in ms]
            inv = 1.0 / functools.reduce(jnp.add, [w * l for w, l in zip(ws, ls)])
            o = functools.reduce(
                jnp.add, [(w * inv) * bf[j].astype(jnp.float32) for w, bf in zip(ws, bufs)]
            )
            att[h][j * BLK : (j + 1) * BLK, :] = o.astype(jnp.bfloat16)
        att_copies(h)

    def att_copies(h):
        def rows(gg):
            return att[h].at[pl.ds(pl.multiple_of(gg * 64, 64), 64), :]

        if h < 2:
            col = pl.ds(pl.multiple_of(y * HD, HD), HD)
            for p in range(2):
                dst = ab[h].at[p, :, col]
                pltpu.make_async_copy(rows(p * 4 + y), dst, tr.at[h]).start()
                for d in (2, 1, 3):
                    yy = lax.rem(y + d, 4)
                    pltpu.make_async_remote_copy(
                        src_ref=rows(p * 4 + yy), dst_ref=dst, send_sem=ts.at[h], recv_sem=tr.at[h],
                        device_id=(b, xh * 4 + yy), device_id_type=MESH,
                    ).start()
        else:
            dst = ab[h].at[:, pl.ds(pl.multiple_of(g * HD, HD), HD)]
            pltpu.make_async_copy(rows(g), dst, tr.at[h]).start()
            for d in range(1, 8):
                gg = head_dev(d)
                pltpu.make_async_remote_copy(
                    src_ref=rows(gg), dst_ref=dst, send_sem=ts.at[h], recv_sem=tr.at[h],
                    device_id=(b, gg), device_id_type=MESH,
                ).start()

    half = w_hbm.shape[1] // 2
    wcol = pl.ds(pl.multiple_of(c * half, 128), half)
    ocol = pl.ds(pl.multiple_of((1 - c) * half, 128), half)
    ydev = {d: (b, xh * 4 + lax.rem(y + d, 4)) for d in (1, 2, 3)}

    def widx(h, d, other=False):
        base = 0 if h < 2 else (1 - xh if other else xh) * 4
        return base + lax.rem(y + d, 4)

    def remote(src_ref, dst_ref, i, dev):
        return pltpu.make_async_remote_copy(
            src_ref=src_ref, dst_ref=dst_ref, send_sem=ws.at[i], recv_sem=wr.at[i], device_id=dev, device_id_type=MESH
        )

    def w_hop1(h, d):
        return remote(
            w_hbm.at[h * HD : (h + 1) * HD, wcol], wb[h].at[widx(h, 0), :, wcol], h * 7 + (0 if d == 1 else 1), ydev[d]
        )

    def w_hop2(h, d):
        ref = wb[h].at[widx(h, 4 - d), pl.ds(0 if d == 1 else 64, 64), wcol]
        return remote(ref, ref, h * 7 + (2 if d == 1 else 3), ydev[d])

    def w_sib(h, d):
        ref = wb[h].at[widx(h, d), :, wcol]
        return remote(ref, ref, h * 7 + 3 + d, plane_dev[1])

    def x_piece(k):
        dst = wb[2].at[widx(2, k), :, wcol]
        return remote(w_hbm.at[2 * HD : 3 * HD, wcol] if k == 0 else dst, dst, 21 + k, xo_dev)

    def x_sib(k):
        ref = wb[2].at[widx(2, k, True), :, wcol]
        return remote(ref, ref, 25 + k, plane_dev[1])

    def w_own(h):
        return pltpu.make_async_copy(w_hbm.at[h * HD : (h + 1) * HD, :], wb[h].at[widx(h, 0)], tr.at[3 + h])

    wsends = []

    def go(cp):
        cp.start()
        wsends.append(cp)

    def w_ready(h):
        w_own(h).wait()
        for d in (1, 2, 3):
            wait_bytes(wb[h].at[widx(h, d), :, ocol], wr.at[h * 7 + 3 + d])
        if h == 2:
            for k in range(4):
                wait_bytes(wb[2].at[widx(2, k, True), :, ocol], wr.at[25 + k])

    step = 768

    def project(k):
        h = min(k, 1)
        if k < 2:
            w_ready(h)
            wait_bytes(ab[h], tr.at[h])
        rows = ab[h][...].reshape(2 * 64, 4 * HD)
        n = pacc.shape[1] // step

        for t in range(*((0, n), (0, n // 2), (n // 2, n))[k]):
            col = slice(t * step, (t + 1) * step)
            res = jnp.dot(rows, wb[h][:, :, col].reshape(4 * HD, step), preferred_element_type=jnp.float32)
            if h:
                res = res + pacc[:, col]
                pb[:, col] = res.astype(jnp.bfloat16)
                p_copy(t).start()
            pacc[:, col] = res

    def p_copy(k):
        return pltpu.make_async_remote_copy(
            src_ref=pb.at[pl.ds(pl.multiple_of((1 - xh) * 64, 64), 64), k * step : (k + 1) * step],
            dst_ref=prec.at[:, k * step : (k + 1) * step],
            send_sem=ts.at[3 + k], recv_sem=tr.at[6 + k], device_id=xh_dev, device_id_type=MESH,
        )

    def out_copy(t):
        return pltpu.make_async_copy(obuf.at[:, t * step : (t + 1) * step], out_ref.at[:, t * step : (t + 1) * step], ts.at[7 + t])

    mine = pl.ds(pl.multiple_of(xh * 64, 64), 64)

    def last_head():
        w_ready(2)
        wait_bytes(ab[2], tr.at[2])
        rows = ab[2][...]
        for t in range(pacc.shape[1] // step):
            col = slice(t * step, (t + 1) * step)
            res = jnp.dot(rows, wb[2][:, :, col].reshape(8 * HD, step), preferred_element_type=jnp.float32)
            total[:, col] = res + pacc[mine, col]

    def final():
        for t in range(pacc.shape[1] // step):
            p_copy(t).wait_recv()
            col = slice(t * step, (t + 1) * step)
            obuf[:, col] = (total[:, col] + prec[:, col].astype(jnp.float32)).astype(jnp.bfloat16)
            out_copy(t).start()

    def job(text):
        if text[:3] == "a2a":
            a2a_start(text[3], int(text[4]))
            return
        if text[0] == "z":
            z_step(text[1], text[2], int(text[3]), int(text[4]))
            return
        if text in ("fin", "final"):
            (last_head if text == "fin" else final)()
            return
        name = next(a for a in NAMES if text.startswith(a))
        v = [int(a) for a in text[len(name) :]]
        if name == "unit":
            unit(*v)
        elif name == "merge":
            merge(*v)
        elif name == "proj":
            project(*v)
        elif name == "qsend":
            q_send(*v)
        elif name == "qfwd":
            q_fwd(*v)
        elif name == "w1":
            go(w_hop1(v[0], 1))
            go(w_hop1(v[0], 3))
        elif name == "w1r":
            h = v[0]
            w_hop1(h, 1).wait_recv()
            w_hop1(h, 3).wait_recv()
            go(w_hop2(h, 1))
            go(w_hop2(h, 3))
            go(w_sib(h, 1))
            go(w_sib(h, 3))
            if h == 2:
                go(x_piece(1))
                go(x_piece(3))
        elif name == "w2r":
            h = v[0]
            w_hop2(h, 1).wait_recv()
            w_hop2(h, 3).wait_recv()
            go(w_sib(h, 2))
            if h == 2:
                go(x_piece(2))
        elif name == "xo":
            go(x_piece(0))
        elif name == "xor":
            k = (0, 1, 3, 2)[v[0]]
            x_piece(k).wait_recv()
            go(x_sib(k))

    kv_own.start()
    for cp in kv_copies:
        cp.start()
    for text in JOBS[:2]:
        job(text)
    for h in range(nh):
        w_own(h).start()
    for text in JOBS[2:]:
        job(text)

    for key in HOPS:
        for direction in "UD":
            zcopy(direction, *key).wait_send()
    for h in range(nh):
        for i in (1, 2, 3):
            q_copy(h, i).wait_send()
            o_copy(h, i).wait_send()
    for (x, h), i in a2a_idx.items():
        wait_bytes(src[x].at[:, pl.ds(0, 7 * HD)], a_send.at[i])
    for cp in wsends:
        cp.wait_send()
    wait_bytes(att[0].at[pl.ds(0, 6 * 64)], ts.at[0])
    wait_bytes(att[1].at[pl.ds(0, 6 * 64)], ts.at[1])
    wait_bytes(att[2].at[pl.ds(0, 7 * 64)], ts.at[2])
    for t in range(pacc.shape[1] // step):
        p_copy(t).wait_send()
        out_copy(t).wait()


def on_device(query_tokens, key_tokens, value_tokens, out_weight, kv_blocks):
    nh = HEADS_DEV
    rows, width = query_tokens.shape
    any_spec = pl.BlockSpec(memory_space=pl.ANY)
    vm = pl.BlockSpec(memory_space=pltpu.VMEM)
    bf = jnp.bfloat16
    dma = pltpu.SemaphoreType.DMA
    return pl.pallas_call(
        kernel,
        out_shape=jax.ShapeDtypeStruct((rows, width), bf),
        in_specs=[any_spec, any_spec, any_spec, any_spec, vm],
        out_specs=any_spec,
        scratch_shapes=[pltpu.VMEM((20, BLK, HD), bf)] * (2 * nh)
        + [pltpu.VMEM((16, BLK, HD), bf)] * nh
        + [pltpu.VMEM((4, 5, BLK, HD), bf)] * (2 * nh)
        + [pltpu.VMEM((n, HD, width), bf) for n in (4, 4, 8)]
        + [pltpu.VMEM((8 * rows, HD), bf)] * nh
        + [pltpu.VMEM((2, rows, 4 * HD), bf)] * 2
        + [pltpu.VMEM((rows, 8 * HD), bf)]
        + [pltpu.VMEM((8, BLK, HD), bf)] * (2 * nh)
        + [
            pltpu.VMEM((4, *kv_blocks.shape), jnp.int32),
            pltpu.SMEM((4, *kv_blocks.shape), jnp.int32),
            pltpu.VMEM((2 * rows, width), jnp.float32),
            pltpu.VMEM((2 * rows, width), bf),
            pltpu.VMEM((rows, width), bf),
            pltpu.VMEM((rows, width), bf),
            pltpu.VMEM((rows, width), jnp.float32),
            dma((9,)), dma((9,)),
            dma((36,)), dma((36,)),
            dma((9,)), dma((9,)),
            dma((12,)), dma((12,)),
            dma((8,)),
            dma((29,)), dma((29,)),
            dma((11,)), dma((10,)),
        ],
        compiler_params=pltpu.CompilerParams(
            collective_id=0, has_side_effects=True, vmem_limit_bytes=60 << 20
        ),
        name="attend",
    )(query_tokens, key_tokens, value_tokens, out_weight, kv_blocks)


def solution(mesh):
    placed = (
        P(("blk", "head"), None),
        P(("blk", "head"), None),
        P(("blk", "head"), None),
        P("head", None),
        P("blk", None),
    )
    return jax.shard_map(
        on_device, mesh=mesh, in_specs=placed, out_specs=P(("blk", "head"), None), check_vma=False
    )
```

```python
import functools
import math

import jax
import jax.numpy as jnp
from jax import lax
from jax.experimental import pallas as pl
from jax.experimental.pallas import tpu as pltpu
from jax.sharding import PartitionSpec as P

HD = 128
BLK = 128
HEADS_DEV = 3
NAMES = ("unit", "merge", "proj", "qsend", "qfwd", "w1r", "w1", "w2r", "xor", "xo")
MESH = pl.DeviceIdType.MESH
ABSENT = -(2.0**100)
SCALE = math.log2(math.e) / math.sqrt(HD)

OWN, M1, P1, M2, P2, MIR, TMP = range(7)
UP = {1: M1, 2: M2, 3: TMP, 4: MIR}
DOWN = {1: P1, 2: P2, 3: TMP, 4: MIR}
HOPS = [(kind, h, hop) for h in range(HEADS_DEV) for kind, n in (("A", 4), ("B", 2)) for hop in range(1, n + 1)]
JOBS = (
    "a2aK0", "a2aV0", "a2aV1", "a2aK1", "a2aQ0", "a2aQ1", "a2aK2", "a2aV2", "a2aQ2", "w10", "w12", "xo0",
    "zDB01", "zUA01", "zDA01", "zUB01", "zDA11", "zUB11", "zUA11", "zDB11", "qsend0", "zDB02", "zUA02",
    "qsend1", "zUA21", "zDB21", "zDA02", "zUB02", "zUB21", "zDA21", "qsend2", "zDA12", "zUB12", "zDB12",
    "zUA12", "qfwd0", "qfwd1", "w11", "zUA03", "qfwd2", "zDB22", "zUA22", "zDA03", "unit03", "unit02",
    "xor0", "zDA22", "zUB22", "unit01", "w1r0", "zDA13", "w1r2", "zUA13", "unit12", "unit13", "unit11",
    "zUA04", "zDA04", "zUA23", "zDA23", "unit22", "w2r0", "unit23", "w1r1", "zDA14", "zUA14", "unit21",
    "w2r2", "unit00", "merge0", "xor1", "xor2", "zDA24", "zUA24", "w2r1", "unit10", "merge1", "proj0",
    "unit20", "merge2", "proj1", "proj2", "xor3", "fin", "final",
)


def kernel(q_hbm, k_hbm, v_hbm, w_hbm, kvb_ref, out_ref, prec, *scratch):
    nh = HEADS_DEV
    kb, vb, qb_, os_, or_, wb, att, ab, km, vm = (scratch[i * nh : (i + 1) * nh] for i in range(10))
    (kvb_all, kvb_smem, pacc, pb, total, a_send, a_recv, zs, zr, qs, qr, osem, orsem, misc, ws, wr, ts, tr) = scratch[10 * nh :]
    b = lax.axis_index("blk")
    g = lax.axis_index("head")
    z, r = lax.div(b, 4), lax.rem(b, 4)
    xl, c = lax.div(r, 2), lax.rem(r, 2)
    ghalf, glow = lax.div(g, 2), lax.rem(g, 2)
    plane = [(xl, c), (xl, 1 - c), (1 - xl, c), (1 - xl, 1 - c)]
    plane_r = [x * 2 + cc for x, cc in plane]
    plane_dev = [(z * 4 + rr, g) for rr in plane_r]
    xh, y = lax.div(g, 4), lax.rem(g, 4)
    xo_dev = (z * 4 + (1 - xl) * 2 + c, (1 - xh) * 4 + y)
    xh_dev = (b, (1 - xh) * 4 + y)
    zdev = {"U": (lax.rem(z + 1, 8) * 4 + r, g), "D": (lax.rem(z + 7, 8) * 4 + r, g)}

    def head_dev(d):
        return lax.rem(g + d, 8)

    barrier = pltpu.get_barrier_semaphore()
    for dev in plane_dev[1:] + list(zdev.values()) + [(b, head_dev(d)) for d in range(1, 8)] + [xo_dev]:
        pl.semaphore_signal(barrier, inc=1, device_id=dev, device_id_type=MESH)
    pl.semaphore_wait(barrier, 13)

    def wait_bytes(ref, sem):
        pltpu.make_async_copy(ref, ref, sem).wait()

    done = set()

    src = {"K": k_hbm, "V": v_hbm, "Q": q_hbm}

    def a2a_dst(x, h):
        if x == "Q":
            return qb_[h], r * 4
        return (kb if x == "K" else vb)[h], OWN * 4

    a2a_idx = {}
    for h in range(nh):
        for x in "KVQ":
            a2a_idx[x, h] = len(a2a_idx)

    def a2a_start(x, h):
        i = a2a_idx[x, h]
        buf, base = a2a_dst(x, h)
        dst = buf.at[base + ghalf, pl.ds(pl.multiple_of(glow * 64, 64), 64), :]

        def cols(dest):
            return src[x].at[:, pl.ds(pl.multiple_of(dest * (nh * HD) + h * HD, HD), HD)]

        pltpu.make_async_copy(cols(g), dst, a_recv.at[i]).start()

        def one(d, carry):
            dest = head_dev(d)
            pltpu.make_async_remote_copy(
                src_ref=cols(dest), dst_ref=dst, send_sem=a_send.at[i], recv_sem=a_recv.at[i],
                device_id=(b, dest), device_id_type=MESH,
            ).start()
            return carry

        lax.fori_loop(1, 8, one, 0)

    def a2a_wait(x, h):
        if ("a2a", x, h) in done:
            return
        done.add(("a2a", x, h))
        buf, base = a2a_dst(x, h)
        wait_bytes(buf.at[pl.ds(base, 4)], a_recv.at[a2a_idx[x, h]])

    kv_copies = []
    for i in range(1, 4):
        kv_copies.append(
            pltpu.make_async_remote_copy(
                src_ref=kvb_ref, dst_ref=kvb_all.at[r], send_sem=misc.at[2 * i], recv_sem=misc.at[2 * i + 1],
                device_id=plane_dev[i], device_id_type=MESH,
            )
        )
    kv_own = pltpu.make_async_copy(kvb_ref, kvb_all.at[r], misc.at[0])


    def tensor(direction, kind):
        return (kb, km) if (direction == "U") == (kind == "A") else (vb, vm)

    def slot_ref(bufs, h, slot):
        return bufs[0][h].at[pl.ds(slot * 4, 4)] if slot < MIR else bufs[1][h].at[pl.ds((slot - MIR) * 4, 4)]

    zname = {}

    def zcopy(direction, kind, h, hop):
        slots = UP if direction == "U" else DOWN
        bufs = tensor(direction, kind)
        s_src = OWN if hop == 1 else slots[hop - 1]
        s_dst = slots[hop]
        k = HOPS.index((kind, h, hop)) + (len(HOPS) if direction == "D" else 0)
        return pltpu.make_async_remote_copy(
            src_ref=slot_ref(bufs, h, s_src), dst_ref=slot_ref(bufs, h, s_dst),
            send_sem=zs.at[k], recv_sem=zr.at[k], device_id=zdev[direction], device_id_type=MESH,
        )

    def z_wait(*key):
        if key not in done:
            done.add(key)
            zcopy(*key).wait_recv()

    def z_step(direction, kind, h, hop):
        if hop == 1:
            is_k = (direction == "U") == (kind == "A")
            a2a_wait("K" if is_k else "V", h)
        else:
            z_wait(direction, kind, h, hop - 1)
        zcopy(direction, kind, h, hop).start()

    def q_copy(h, i):
        ref = qb_[h].at[pl.ds(plane_r[2 if i == 3 else 0] * 4, 4)]
        return pltpu.make_async_remote_copy(
            src_ref=ref, dst_ref=ref, send_sem=qs.at[h * 3 + i - 1], recv_sem=qr.at[h * 3 + i - 1],
            device_id=plane_dev[2 if i == 2 else 1], device_id_type=MESH,
        )

    def q_send(h):
        a2a_wait("Q", h)
        for i in (2, 1):
            q_copy(h, i).start()

    def q_fwd(h):
        q_wait(h, (2,))
        q_copy(h, 3).start()

    def q_wait(h, which=(1, 2, 3)):
        for i in which:
            if ("q", h, i) not in done:
                done.add(("q", h, i))
                wait_bytes(qb_[h].at[pl.ds(plane_r[i] * 4, 4)], qr.at[h * 3 + i - 1])

    def kvb_wait():
        if "kvb" in done:
            return
        done.add("kvb")
        kv_own.wait()
        for i in range(1, 4):
            kv_copies[i - 1].wait()
        cp = pltpu.make_async_copy(kvb_all, kvb_smem, misc.at[1])
        cp.start()
        cp.wait()

    lane = lax.broadcasted_iota(jnp.int32, (BLK, BLK), 1)
    ones = jnp.ones((BLK, HD), jnp.bfloat16)

    def o_copy(h, i):
        return pltpu.make_async_remote_copy(
            src_ref=os_[h].at[i], dst_ref=or_[h].at[i], send_sem=osem.at[h * 4 + i], recv_sem=orsem.at[h * 4 + i],
            device_id=plane_dev[i], device_id_type=MESH,
        )

    def unit(h, i):
        kvb_wait()
        q_wait(h)
        for x in "KV":
            a2a_wait(x, h)
        for kind, hh, hop in HOPS:
            if hh == h and hop in ((1, 2, 4) if i == 0 else (1, 2)):
                z_wait("U", kind, h, hop)
                z_wait("D", kind, h, hop)
        rq = plane_r[i]
        dl = r - rq
        gt = lax.div(dl + 3, 4)
        lt = lax.div(3 - dl, 4)
        eq = 1 - gt - lt
        picks = [
            (OWN, gt * (2 * dl) + lt * (1 - 2 * dl)),
            (M1, 9 - 2 * dl),
            (P1, 2 * dl + 8),
            (0 if i == 0 else M2 * gt + P2 * lt, gt * (17 - 2 * dl) + lt * (2 * dl + 16) + eq),
        ]

        def block(j, stats):
            q = qb_[h][rq * 4 + j]
            scores, vals = [], []
            for n, (slot, col) in enumerate(picks):
                keys, values = (km[h], vm[h]) if n == 3 and i == 0 else (kb[h], vb[h])
                e = kvb_smem[rq, j, col]
                idx = slot * 4 + jnp.bitwise_and(e, 3)
                bias = jnp.where(e >= 0, 0.0, ABSENT).astype(jnp.float32)
                s = lax.dot_general(q, keys[idx], (((1,), (1,)), ((), ())), preferred_element_type=jnp.float32)
                scores.append(s * SCALE + bias)
                vals.append(jnp.concatenate([values[idx], ones], axis=1))
            top = functools.reduce(jnp.maximum, scores)
            m = jnp.max(top, axis=1, keepdims=True).astype(jnp.bfloat16).astype(jnp.float32)
            ps = [jnp.exp2(s - m).astype(jnp.bfloat16) for s in scores]
            o = functools.reduce(
                jnp.add,
                [jnp.dot(p, v, preferred_element_type=jnp.float32) for p, v in zip(ps, vals)],
            )
            os_[h][i, j] = o[:, :HD].astype(jnp.bfloat16)
            l = o[:, HD:]
            l_hi = l.astype(jnp.bfloat16).astype(jnp.float32)
            stats = jnp.where(lane == j, m, stats)
            stats = jnp.where(lane == j + 4, l_hi, stats)
            return jnp.where(lane == j + 8, l - l_hi, stats)

        stats = lax.fori_loop(0, 4, block, jnp.zeros((BLK, BLK), jnp.float32), unroll=4)
        os_[h][i, 4] = stats.astype(jnp.bfloat16)
        if i:
            o_copy(h, i).start()

    def merge(h):
        for i in (1, 2, 3):
            o_copy(h, i).wait_recv()
        bufs = [os_[h].at[0]] + [or_[h].at[i] for i in (1, 2, 3)]
        stats = [bf[4].astype(jnp.float32) for bf in bufs]
        for j in range(4):
            ms = [s[:, j : j + 1] for s in stats]
            ls = [s[:, j + 4 : j + 5] + s[:, j + 8 : j + 9] for s in stats]
            top = functools.reduce(jnp.maximum, ms)
            ws = [jnp.exp2(m - top) for m in ms]
            inv = 1.0 / functools.reduce(jnp.add, [w * l for w, l in zip(ws, ls)])
            o = functools.reduce(
                jnp.add, [(w * inv) * bf[j].astype(jnp.float32) for w, bf in zip(ws, bufs)]
            )
            att[h][j * BLK : (j + 1) * BLK, :] = o.astype(jnp.bfloat16)
        att_copies(h)

    def att_copies(h):
        def rows(gg):
            return att[h].at[pl.ds(pl.multiple_of(gg * 64, 64), 64), :]

        if h < 2:
            col = pl.ds(pl.multiple_of(y * HD, HD), HD)
            for p in range(2):
                dst = ab[h].at[p, :, col]
                pltpu.make_async_copy(rows(p * 4 + y), dst, tr.at[h]).start()
                for d in (2, 1, 3):
                    yy = lax.rem(y + d, 4)
                    pltpu.make_async_remote_copy(
                        src_ref=rows(p * 4 + yy), dst_ref=dst, send_sem=ts.at[h], recv_sem=tr.at[h],
                        device_id=(b, xh * 4 + yy), device_id_type=MESH,
                    ).start()
        else:
            dst = ab[h].at[:, pl.ds(pl.multiple_of(g * HD, HD), HD)]
            pltpu.make_async_copy(rows(g), dst, tr.at[h]).start()
            for d in range(1, 8):
                gg = head_dev(d)
                pltpu.make_async_remote_copy(
                    src_ref=rows(gg), dst_ref=dst, send_sem=ts.at[h], recv_sem=tr.at[h],
                    device_id=(b, gg), device_id_type=MESH,
                ).start()

    half = w_hbm.shape[1] // 2
    wcol = pl.ds(pl.multiple_of(c * half, 128), half)
    ocol = pl.ds(pl.multiple_of((1 - c) * half, 128), half)
    ydev = {d: (b, xh * 4 + lax.rem(y + d, 4)) for d in (1, 2, 3)}

    def widx(h, d, other=False):
        base = 0 if h < 2 else (1 - xh if other else xh) * 4
        return base + lax.rem(y + d, 4)

    def remote(src_ref, dst_ref, i, dev):
        return pltpu.make_async_remote_copy(
            src_ref=src_ref, dst_ref=dst_ref, send_sem=ws.at[i], recv_sem=wr.at[i], device_id=dev, device_id_type=MESH
        )

    def w_hop1(h, d):
        return remote(
            w_hbm.at[h * HD : (h + 1) * HD, wcol], wb[h].at[widx(h, 0), :, wcol], h * 7 + (0 if d == 1 else 1), ydev[d]
        )

    def w_hop2(h, d):
        ref = wb[h].at[widx(h, 4 - d), pl.ds(0 if d == 1 else 64, 64), wcol]
        return remote(ref, ref, h * 7 + (2 if d == 1 else 3), ydev[d])

    def w_sib(h, d):
        ref = wb[h].at[widx(h, d), :, wcol]
        return remote(ref, ref, h * 7 + 3 + d, plane_dev[1])

    def x_piece(k):
        dst = wb[2].at[widx(2, k), :, wcol]
        return remote(w_hbm.at[2 * HD : 3 * HD, wcol] if k == 0 else dst, dst, 21 + k, xo_dev)

    def x_sib(k):
        ref = wb[2].at[widx(2, k, True), :, wcol]
        return remote(ref, ref, 25 + k, plane_dev[1])

    def w_own(h):
        return pltpu.make_async_copy(w_hbm.at[h * HD : (h + 1) * HD, :], wb[h].at[widx(h, 0)], tr.at[3 + h])

    wsends = []

    def go(cp):
        cp.start()
        wsends.append(cp)

    def w_ready(h):
        w_own(h).wait()
        for d in (1, 2, 3):
            wait_bytes(wb[h].at[widx(h, d), :, ocol], wr.at[h * 7 + 3 + d])
        if h == 2:
            for k in range(4):
                wait_bytes(wb[2].at[widx(2, k, True), :, ocol], wr.at[25 + k])

    step = 768

    def project(k):
        h = min(k, 1)
        if k < 2:
            w_ready(h)
            wait_bytes(ab[h], tr.at[h])
        rows = ab[h][...].reshape(2 * 64, 4 * HD)
        n = pacc.shape[1] // step

        for t in range(*((0, n), (0, n // 2), (n // 2, n))[k]):
            col = slice(t * step, (t + 1) * step)
            res = jnp.dot(rows, wb[h][:, :, col].reshape(4 * HD, step), preferred_element_type=jnp.float32)
            if h:
                res = res + pacc[:, col]
                pb[:, col] = res.astype(jnp.bfloat16)
                p_copy(t).start()
            pacc[:, col] = res

    def p_copy(k):
        return pltpu.make_async_remote_copy(
            src_ref=pb.at[pl.ds(pl.multiple_of((1 - xh) * 64, 64), 64), k * step : (k + 1) * step],
            dst_ref=prec.at[:, k * step : (k + 1) * step],
            send_sem=ts.at[3 + k], recv_sem=tr.at[6 + k], device_id=xh_dev, device_id_type=MESH,
        )

    def out_copy(t):
        return pltpu.make_async_copy(total.at[:, t * step : (t + 1) * step], out_ref.at[:, t * step : (t + 1) * step], ts.at[7 + t])

    mine = pl.ds(pl.multiple_of(xh * 64, 64), 64)

    def last_head():
        w_ready(2)
        wait_bytes(ab[2], tr.at[2])
        rows = ab[2][...]
        for t in range(pacc.shape[1] // step):
            col = slice(t * step, (t + 1) * step)
            res = jnp.dot(rows, wb[2][:, :, col].reshape(8 * HD, step), preferred_element_type=jnp.float32)
            total[:, col] = res + pacc[mine, col]
            out_copy(t).start()

    def final():
        for t in range(pacc.shape[1] // step):
            p_copy(t).wait_recv()

    def job(text):
        if text[:3] == "a2a":
            a2a_start(text[3], int(text[4]))
            return
        if text[0] == "z":
            z_step(text[1], text[2], int(text[3]), int(text[4]))
            return
        if text in ("fin", "final"):
            (last_head if text == "fin" else final)()
            return
        name = next(a for a in NAMES if text.startswith(a))
        v = [int(a) for a in text[len(name) :]]
        if name == "unit":
            unit(*v)
        elif name == "merge":
            merge(*v)
        elif name == "proj":
            project(*v)
        elif name == "qsend":
            q_send(*v)
        elif name == "qfwd":
            q_fwd(*v)
        elif name == "w1":
            go(w_hop1(v[0], 1))
            go(w_hop1(v[0], 3))
        elif name == "w1r":
            h = v[0]
            w_hop1(h, 1).wait_recv()
            w_hop1(h, 3).wait_recv()
            go(w_hop2(h, 1))
            go(w_hop2(h, 3))
            go(w_sib(h, 1))
            go(w_sib(h, 3))
            if h == 2:
                go(x_piece(1))
                go(x_piece(3))
        elif name == "w2r":
            h = v[0]
            w_hop2(h, 1).wait_recv()
            w_hop2(h, 3).wait_recv()
            go(w_sib(h, 2))
            if h == 2:
                go(x_piece(2))
        elif name == "xo":
            go(x_piece(0))
        elif name == "xor":
            k = (0, 1, 3, 2)[v[0]]
            x_piece(k).wait_recv()
            go(x_sib(k))

    kv_own.start()
    for cp in kv_copies:
        cp.start()
    for text in JOBS[:2]:
        job(text)
    for h in range(nh):
        w_own(h).start()
    for text in JOBS[2:]:
        job(text)

    for key in HOPS:
        for direction in "UD":
            zcopy(direction, *key).wait_send()
    for h in range(nh):
        for i in (1, 2, 3):
            q_copy(h, i).wait_send()
            o_copy(h, i).wait_send()
    for (x, h), i in a2a_idx.items():
        wait_bytes(src[x].at[:, pl.ds(0, 7 * HD)], a_send.at[i])
    for cp in wsends:
        cp.wait_send()
    wait_bytes(att[0].at[pl.ds(0, 6 * 64)], ts.at[0])
    wait_bytes(att[1].at[pl.ds(0, 6 * 64)], ts.at[1])
    wait_bytes(att[2].at[pl.ds(0, 7 * 64)], ts.at[2])
    for t in range(pacc.shape[1] // step):
        p_copy(t).wait_send()
        out_copy(t).wait()


def on_device(query_tokens, key_tokens, value_tokens, out_weight, kv_blocks):
    nh = HEADS_DEV
    rows, width = query_tokens.shape
    any_spec = pl.BlockSpec(memory_space=pl.ANY)
    vm = pl.BlockSpec(memory_space=pltpu.VMEM)
    bf = jnp.bfloat16
    dma = pltpu.SemaphoreType.DMA
    total, other = pl.pallas_call(
        kernel,
        out_shape=(jax.ShapeDtypeStruct((rows, width), jnp.float32), jax.ShapeDtypeStruct((rows, width), bf)),
        in_specs=[any_spec, any_spec, any_spec, any_spec, vm],
        out_specs=(any_spec, any_spec),
        scratch_shapes=[pltpu.VMEM((20, BLK, HD), bf)] * (2 * nh)
        + [pltpu.VMEM((16, BLK, HD), bf)] * nh
        + [pltpu.VMEM((4, 5, BLK, HD), bf)] * (2 * nh)
        + [pltpu.VMEM((n, HD, width), bf) for n in (4, 4, 8)]
        + [pltpu.VMEM((8 * rows, HD), bf)] * nh
        + [pltpu.VMEM((2, rows, 4 * HD), bf)] * 2
        + [pltpu.VMEM((rows, 8 * HD), bf)]
        + [pltpu.VMEM((8, BLK, HD), bf)] * (2 * nh)
        + [
            pltpu.VMEM((4, *kv_blocks.shape), jnp.int32),
            pltpu.SMEM((4, *kv_blocks.shape), jnp.int32),
            pltpu.VMEM((2 * rows, width), jnp.float32),
            pltpu.VMEM((2 * rows, width), bf),
            pltpu.VMEM((rows, width), jnp.float32),
            dma((9,)), dma((9,)),
            dma((36,)), dma((36,)),
            dma((9,)), dma((9,)),
            dma((12,)), dma((12,)),
            dma((8,)),
            dma((29,)), dma((29,)),
            dma((11,)), dma((10,)),
        ],
        compiler_params=pltpu.CompilerParams(
            collective_id=0, has_side_effects=True, vmem_limit_bytes=60 << 20
        ),
        name="attend",
    )(query_tokens, key_tokens, value_tokens, out_weight, kv_blocks)
    return (total + other.astype(jnp.float32)).astype(bf)


def solution(mesh):
    placed = (
        P(("blk", "head"), None),
        P(("blk", "head"), None),
        P(("blk", "head"), None),
        P("head", None),
        P("blk", None),
    )
    return jax.shard_map(
        on_device, mesh=mesh, in_specs=placed, out_specs=P(("blk", "head"), None), check_vma=False
    )
```
